32 devices in a mesh: worker: 4 (over x, core), outer: 4 (over z), mp: 2 (over y).
Axes of the slice: x: 2, y: 2, z: 4, core: 2. Of those that a mesh axis runs over, the one named last changes fastest.
Arguments:
- grads: float32 [4, 4, 3584, 4096], P('worker', 'outer', None, 'mp'), as said below
- center: float32 [3584, 4096], P(('worker', 'outer'), 'mp'), may hold values from -6 to 6
- radius: float32 [1], replicated, may hold values from 1.5 to 3.5
Outputs:
- center_out: float32 [3584, 4096], P(('worker', 'outer'), 'mp')
The draws below stay inside these ranges and needn't reach their ends.
Inputs may be any that keep to these rules, and one draw needn't show every extreme that they name: `grads`: finite values.
All inputs are finite; a program needn't handle non-finite values.
Results may differ from the reference program's by a relative error of at most 0.0001.
Values sent between devices are 32-bit elements; how exact they have to be, the bound alone decides.
No kernel may reach another device: no remote copies, remote signals or barrier semaphores. Data moves between devices by JAX's collectives and lax.ppermute only.
A program may use at most 192 MiB of HBM per device.

```python
import math
import jax
import jax.numpy as jnp
from jax import lax

D = 3584
ITERS = 2
KVW = 4096
N_WORKER = 4
N_OUTER = 4


def draw_grads(key, part):
    keys = jax.random.split(key, 4)
    worker_scale = jnp.exp(jax.random.uniform(keys[0], (N_WORKER, N_OUTER, 1, 1), jnp.float32, math.log(0.4), math.log(4.0)))
    row_scale = jnp.exp(jax.random.uniform(keys[1], (1, 1, D, 1), jnp.float32, math.log(0.3), math.log(3.0)))
    columns = jnp.arange(KVW, dtype=jnp.float32) / KVW - 0.5
    trend = jnp.exp(math.log(3.0) * columns).reshape(1, 1, 1, KVW)
    column_scale = trend * jnp.exp(jax.random.uniform(keys[2], (1, 1, 1, KVW), jnp.float32, math.log(0.5), math.log(2.0)))
    shape = (N_WORKER, N_OUTER, D, KVW)
    noise = jax.random.normal(keys[3], shape, jnp.float32)
    return (worker_scale * row_scale * column_scale * noise).astype(jnp.float32)


def steps_of(own_key, dims, shards, smallest, top_value):
    factor_of, own = 1.0, jax.random.fold_in(own_key, 6)
    for position, shards_of in shards:
        steps = jnp.exp(jax.random.uniform(jax.random.fold_in(own, position), (shards_of,), jnp.float32, smallest / len(shards), top_value / len(shards)))
        factor_of = factor_of * jnp.repeat(steps, dims[position] // shards_of).reshape([-1 if axis == position else 1 for axis in range(len(dims))])
    return factor_of


def normal_values(stream_key, extent, deviation, most, pieces=(), held_as=jnp.bfloat16):
    result = jax.random.normal(stream_key, extent, jnp.float32) * deviation
    if len(pieces) > 0:
        result = steps_of(stream_key, extent, pieces, -0.22, 0.18) * result
    return jnp.clip(result, min=-most, max=most).astype(held_as)


def setup_inputs(seed: int = 0) -> dict:
    streams_of = jax.random.split(jax.random.key(seed), 4)
    grads = draw_grads(jax.random.fold_in(streams_of[3], 71), 0)
    center = normal_values(streams_of[1], (D, KVW), 1.0, 6.0, ((0, 16), (1, 2)), jnp.float32)
    radius = jnp.clip(jax.random.uniform(streams_of[2], (1,), jnp.float32, 1.5, 3.5), 1.5, 3.5)
    return dict(grads=grads, center=center, radius=radius)


epsilon = 1e-06

def reference(grads, center, radius):
    per_worker = grads.reshape(N_WORKER * N_OUTER, D, KVW)
    radius_total = radius[0] * math.sqrt(D * KVW)
    current = center
    for iteration in range(ITERS):

        def accumulate(summed, gradient):
            difference = gradient - current
            squares = jnp.sum(difference * difference)
            factor = jnp.minimum(1.0, radius_total * lax.rsqrt(squares + epsilon))
            return (summed + factor * difference, None)
        summed, unused = lax.scan(accumulate, jnp.zeros_like(center), per_worker)
        current = current + summed / (N_WORKER * N_OUTER)
    return current
```

```python
import math

import jax
import jax.numpy as jnp
from jax import lax
from jax.sharding import PartitionSpec as P

D = 3584
ITERS = 2
KVW = 4096
AXES = ("worker", "outer", "mp")

epsilon = 1e-06


def sum_over_devices(value):
    for axis in AXES:
        size = lax.axis_size(axis)
        step = 1
        while step < size:
            value = value + lax.ppermute(value, axis, [(i, i ^ step) for i in range(size)])
            step *= 2
    return value


def on_device(grads, center, radius):
    worker_count = lax.axis_size("worker") * lax.axis_size("outer")
    radius_total = radius[0] * math.sqrt(D * KVW)
    own_rows = center
    mine = grads.reshape(worker_count, grads.shape[2] // worker_count, grads.shape[3])
    gathered = lax.all_to_all(mine, ("worker", "outer"), split_axis=0, concat_axis=0, tiled=True)
    for iteration in range(ITERS):
        difference = gathered - own_rows[None]
        partial_value = jnp.sum(difference * difference, axis=(1, 2))
        norm_sq = sum_over_devices(partial_value)
        factor = jnp.minimum(1.0, radius_total * lax.rsqrt(norm_sq + epsilon))
        summed = jnp.sum(factor[:, None, None] * difference, axis=0)
        own_rows = own_rows + summed / worker_count
    return own_rows


def solution(mesh):
    in_specs = (P("worker", "outer", None, "mp"), P(("worker", "outer"), "mp"), P())
    out_specs = P(("worker", "outer"), "mp")
    return jax.shard_map(
        on_device, mesh=mesh, in_specs=in_specs, out_specs=out_specs, check_vma=False
    )
```

```python
import math

import jax
import jax.numpy as jnp
from jax import lax
from jax.sharding import PartitionSpec as P

D = 3584
ITERS = 2
KVW = 4096
AXES = ("worker", "outer", "mp")
LINE = 4
SPREAD = 3 / 7
CHUNKS = 8

epsilon = 1e-06


def sum_over_devices(value):
    for axis in AXES:
        size = lax.axis_size(axis)
        step = 1
        while step < size:
            value = value + lax.ppermute(value, axis, [(i, i ^ step) for i in range(size)])
            step *= 2
    return value


def to_mids(value):
    return lax.ppermute(value, "outer", [(0, 1), (3, 2)])


def across(value):
    return lax.ppermute(value, "outer", [(1, 2), (2, 1)])


def to_ends(value):
    return lax.ppermute(value, "outer", [(1, 0), (2, 3)])


def spread_only(mine, center, radius_total, worker_count):
    own_rows = center
    gathered = lax.all_to_all(mine, ("worker", "outer"), split_axis=0, concat_axis=0, tiled=True)
    for iteration in range(ITERS):
        difference = gathered - own_rows[None]
        norm_sq = sum_over_devices(jnp.sum(difference * difference, axis=(1, 2)))
        factor = jnp.minimum(1.0, radius_total * lax.rsqrt(norm_sq + epsilon))
        own_rows = own_rows + jnp.sum(factor[:, None, None] * difference, axis=0) / worker_count
    return own_rows


def on_device(grads, center, radius):
    workers, outers = lax.axis_size("worker"), lax.axis_size("outer")
    worker_count = workers * outers
    radius_total = radius[0] * math.sqrt(D * KVW)
    rows, columns = center.shape
    mine = grads.reshape(worker_count, rows, columns)
    cut = int(rows * SPREAD) // 16 * 16
    if outers != LINE or workers & (workers - 1) or (rows - cut) % (8 * CHUNKS):
        return spread_only(mine, center, radius_total, worker_count)

    w, o = lax.axis_index("worker"), lax.axis_index("outer")
    is_end = (o == 0) | (o == LINE - 1)
    is_low = o < LINE // 2
    rest = rows - cut

    def line_rows(worker):
        blocks = lax.dynamic_slice(
            mine, (worker * outers, cut, 0), (outers, rest, columns)
        )
        return jnp.where(is_low, blocks[::-1], blocks)

    tail = center[cut:]
    pair = to_pair = lax.ppermute(tail, "outer", [(i, i ^ 1) for i in range(LINE)])
    held = [line_rows(w)]
    for step in range(workers - 1, 0, -1):
        swap = [(i, i ^ step) for i in range(workers)]
        held.append(lax.ppermute(line_rows(w ^ step), "worker", swap))
    steps = [0] + list(range(workers - 1, 0, -1))
    spread = lax.all_to_all(
        mine[:, :cut], ("worker", "outer"), split_axis=0, concat_axis=0, tiled=True
    )
    near = jnp.where(is_end, jnp.stack([pair, tail]), jnp.stack([tail, pair]))
    crossed = across(near)
    far = jnp.where(is_end, to_ends(crossed), crossed)
    line_v = jnp.concatenate([far[::-1], near])
    spread_v = center[:cut]

    places = jnp.stack([(w ^ step) * outers + o for step in steps])
    hit = places[:, None] == jnp.arange(worker_count)[None]

    def factors(spread_sq, line_sq):
        both = spread_sq + jnp.sum(jnp.where(hit, line_sq[:, None], 0.0), axis=0)
        norm_sq = sum_over_devices(both)
        factor = jnp.minimum(1.0, radius_total * lax.rsqrt(norm_sq + epsilon))
        return factor, jnp.sum(jnp.where(hit, factor[None], 0.0), axis=1)

    def spread_norms(v):
        difference = spread - v[None]
        return jnp.sum(difference * difference, axis=(1, 2))

    def spread_update(v, factor):
        return v + jnp.sum(factor[:, None, None] * (spread - v[None]), axis=0) / worker_count

    def line_norms(values, v):
        return jnp.stack([jnp.sum(jnp.square(value - v)) for value in values])

    def line_step(values, v, factor):
        return sum(factor[i] * (value - v) for i, value in enumerate(values))

    factor, line_factor = factors(spread_norms(spread_v), line_norms(held, line_v))

    size = rest // CHUNKS
    pieces, line_sq = [], 0.0
    for chunk in range(CHUNKS):
        part = slice(chunk * size, (chunk + 1) * size)
        values, v = [value[:, part] for value in held], line_v[:, part]
        own = line_step(values, v, line_factor)
        own = own + to_mids(own)
        own = own + across(own)[::-1]
        own = jnp.where(is_end, to_ends(own), own)
        v = v + own / worker_count
        line_sq = line_sq + line_norms(values, v)
        pieces.append(v)
    spread_v = spread_update(spread_v, factor)
    line_v = jnp.concatenate(pieces, axis=1)

    factor, line_factor = factors(spread_norms(spread_v), line_sq)

    block = [
        line_step([value[i] for value in held], line_v[i], line_factor) for i in range(LINE)
    ]
    arrived = [to_mids(block[i]) for i in range(3)]
    passed = [across(block[i] + arrived[i]) for i in range(2)]
    end_sum = block[3] + to_ends(block[3] + passed[0])
    mid_sum = block[2] + arrived[2] + passed[1]
    own_v = jnp.where(is_end, line_v[3], line_v[2])
    own_v = own_v + jnp.where(is_end, end_sum, mid_sum) / worker_count
    return jnp.concatenate([spread_update(spread_v, factor), own_v])


def solution(mesh):
    in_specs = (P("worker", "outer", None, "mp"), P(("worker", "outer"), "mp"), P())
    out_specs = P(("worker", "outer"), "mp")
    return jax.shard_map(
        on_device, mesh=mesh, in_specs=in_specs, out_specs=out_specs, check_vma=False
    )
```

```python
import math

import jax
import jax.numpy as jnp
from jax import lax
from jax.sharding import PartitionSpec as P


D = 3584
ITERS = 2
KVW = 4096
AXES = ("worker", "outer", "mp")
LINE = 4
TILE = 8
SPREAD = 0.4

epsilon = 1e-06


def sum_over_devices(value):
    for axis in AXES:
        size = lax.axis_size(axis)
        step = 1
        while step < size:
            value = value + lax.ppermute(value, axis, [(i, i ^ step) for i in range(size)])
            step *= 2
    return value


def send(value, pairs, axis="outer"):
    return lax.ppermute(value, axis, pairs)


TO_MIDS = [(0, 1), (3, 2)]
ACROSS = [(1, 2), (2, 1)]
TO_ENDS = [(1, 0), (2, 3)]


def tie(value, earlier):
    return lax.optimization_barrier((value, earlier))[0]


def split(rows, outers):
    cut = int(rows * SPREAD) // TILE * TILE
    tiles = (rows - cut) // TILE
    if outers != LINE or (rows - cut) % TILE or tiles < 8:
        return None
    body = tiles - 4
    sizes = [1, 1] + [2] * (body // 2) + [1] * (body % 2) + [1, 1]
    return cut, [size * TILE for size in sizes]


def spread_only(mine, center, radius_total, worker_count):
    own_rows = center
    gathered = lax.all_to_all(mine, ("worker", "outer"), split_axis=0, concat_axis=0, tiled=True)
    for _ in range(ITERS):
        difference = gathered - own_rows[None]
        norm_sq = sum_over_devices(jnp.sum(difference * difference, axis=(1, 2)))
        factor = jnp.minimum(1.0, radius_total * lax.rsqrt(norm_sq + epsilon))
        own_rows = own_rows + jnp.sum(factor[:, None, None] * difference, axis=0) / worker_count
    return own_rows


def on_device(grads, center, radius):
    workers, outers = lax.axis_size("worker"), lax.axis_size("outer")
    worker_count = workers * outers
    radius_total = radius[0] * math.sqrt(D * KVW)
    rows, columns = center.shape
    mine = grads.reshape(worker_count, rows, columns)
    plan = split(rows, outers)
    if plan is None:
        return spread_only(mine, center, radius_total, worker_count)
    cut, sizes = plan
    rest = rows - cut

    w, o = lax.axis_index("worker"), lax.axis_index("outer")
    is_end = (o == 0) | (o == LINE - 1)
    is_low = o < LINE // 2

    def line_rows(source, worker):
        return lax.dynamic_slice(source, (worker * outers, cut, 0), (outers, rest, columns))

    tail = center[cut:]
    pair = send(tail, [(i, i ^ 1) for i in range(LINE)])
    steps = list(range(workers // 2, workers)) + list(range(1, workers // 2)) + [0]
    held, source = [], mine
    for step in steps:
        sent = line_rows(source, w ^ step)
        source = tie(source, sent)
        if step:
            swap = [(i, i ^ step) for i in range(workers)]
            sent = send(sent, swap, "worker")
        held.append(sent)
    spread = lax.all_to_all(
        mine[:, :cut], ("worker", "outer"), split_axis=0, concat_axis=0, tiled=True
    )
    first = (o % 2) == 0
    near = jnp.where(first, jnp.stack([tail, pair]), jnp.stack([pair, tail]))
    crossed = send(near, ACROSS)
    far = jnp.where(is_end, send(crossed, TO_ENDS), crossed)
    line_v = jnp.where(is_low, jnp.concatenate([near, far]), jnp.concatenate([far, near]))
    spread_v = center[:cut]

    places = [(w ^ step) * outers + o for step in steps]
    numbers = jnp.arange(worker_count)

    def factors(spread_sq, line_sq):
        both = spread_sq
        for place, value in zip(places, line_sq):
            both = both + jnp.where(numbers == place, value, 0.0)
        norm_sq = sum_over_devices(both)
        factor = jnp.minimum(1.0, radius_total * lax.rsqrt(norm_sq + epsilon))
        return factor, [jnp.sum(jnp.where(numbers == place, factor, 0.0)) for place in places]

    def spread_norms(v):
        difference = spread - v[None]
        return jnp.sum(difference * difference, axis=(1, 2))

    def spread_update(v, factor):
        return v + jnp.sum(factor[:, None, None] * (spread - v[None]), axis=0) / worker_count

    def line_step(values, v, factor):
        return sum(factor[i] * (value - v) for i, value in enumerate(values))

    line_sq, v = [None] * workers, line_v
    for place in reversed(range(workers)):
        line_sq[place] = jnp.sum(jnp.square(held[place] - v))
        v = tie(v, line_sq[place])
    factor, line_factor = factors(spread_norms(spread_v), line_sq)

    starts = [sum(sizes[:i]) for i in range(len(sizes))]
    pieces, sums = [], [[0.0] * workers]
    for chunk, (start, size) in enumerate(zip(starts, sizes)):
        part = slice(start, start + size)
        values, v = [value[:, part] for value in held], line_v[:, part]
        own = line_step(values, v, line_factor)
        own = own + send(own, TO_MIDS)
        own = own + send(own, ACROSS)
        if chunk >= 3:
            own = tie(own, sums[chunk - 2])
        own = jnp.where(is_end, send(own, TO_ENDS), own)
        v = v + own / worker_count
        sums.append(
            [
                total + jnp.sum(jnp.square(value - v), axis=(0, 1))
                for total, value in zip(sums[-1], values)
            ]
        )
        pieces.append(v)
    spread_v = spread_update(spread_v, factor)
    line_v = jnp.concatenate(pieces, axis=1)
    factor, line_factor = factors(spread_norms(spread_v), [jnp.sum(total) for total in sums[-1]])

    def at(value, place):
        index = jnp.where(is_low, LINE - 1 - place, place)
        return lax.dynamic_index_in_dim(value, index, 0, keepdims=False)

    block, v = [], line_v
    for place in range(LINE):
        block.append(line_step([at(value, place) for value in held], at(v, place), line_factor))
        v = tie(v, block[place])
    arrived = [send(block[place], TO_MIDS) for place in range(3)]
    passed = [send(block[place] + arrived[place], ACROSS) for place in range(2)]
    end_sum = block[3] + send(block[3] + passed[0], TO_ENDS)
    mid_sum = block[2] + arrived[2] + passed[1]
    own_v = lax.dynamic_index_in_dim(line_v, o, 0, keepdims=False)
    own_v = own_v + jnp.where(is_end, end_sum, mid_sum) / worker_count
    return jnp.concatenate([spread_update(spread_v, factor), own_v])


def solution(mesh):
    in_specs = (P("worker", "outer", None, "mp"), P(("worker", "outer"), "mp"), P())
    out_specs = P(("worker", "outer"), "mp")

    return jax.shard_map(on_device, mesh=mesh, in_specs=in_specs, out_specs=out_specs, check_vma=False)
```

```python
import math

import jax
import jax.numpy as jnp
from jax import lax
from jax.experimental import pallas as pl
from jax.experimental.pallas import tpu as pltpu
from jax.sharding import PartitionSpec as P


D = 3584
ITERS = 2
KVW = 4096
AXES = ("worker", "outer", "mp")
LINE = 4
TILE = 8
SPREAD = 0.4

epsilon = 1e-06


def sum_over_devices(value):
    for axis in AXES:
        size = lax.axis_size(axis)
        step = 1
        while step < size:
            value = value + lax.ppermute(value, axis, [(i, i ^ step) for i in range(size)])
            step *= 2
    return value


def send(value, pairs, axis="outer"):
    return lax.ppermute(value, axis, pairs)


TO_MIDS = [(0, 1), (3, 2)]
ACROSS = [(1, 2), (2, 1)]
TO_ENDS = [(1, 0), (2, 3)]


def tie(value, earlier):
    return lax.optimization_barrier((value, earlier))[0]


def split(rows, outers):
    cut = int(rows * SPREAD) // TILE * TILE
    rest = rows - cut
    if outers != LINE or rest % TILE or rest // TILE < 12:
        return None
    tiles = rest // TILE
    body = tiles - 4
    sizes = [1, 2] + [3] * (body // 3) + [body % 3] * (body % 3 > 0) + [1]
    return cut, sizes


SMEM = pl.BlockSpec(memory_space=pltpu.SMEM)


def tiles_at(start, shape):
    return pl.BlockSpec(shape, lambda i: (start + i, 0))


def run(kernel, grid, in_specs, out_specs, out_shape, operands, moved, aliases={}, prefetch=0):
    return pl.pallas_call(
        kernel,
        grid_spec=pltpu.PrefetchScalarGridSpec(
            num_scalar_prefetch=prefetch, grid=grid, in_specs=in_specs, out_specs=out_specs
        ),
        out_shape=out_shape,
        input_output_aliases=aliases,
        compiler_params=pltpu.CompilerParams(vmem_limit_bytes=24 << 20),
        cost_estimate=pl.CostEstimate(flops=4 * moved, bytes_accessed=4 * moved, transcendentals=0),
    )(*operands)


def step_of(factor, values, v):
    return sum(factor[i] * (value[...] - v) for i, value in enumerate(values))


def step_chunk(factor, values, v, start, tiles):
    columns, tile = v.shape[1], TILE * LINE

    def kernel(factor, *refs):
        *values, v, out = refs
        out[...] = step_of(factor, values, v[...])

    at, own = tiles_at(start, (tile, columns)), tiles_at(0, (tile, columns))
    shape = jax.ShapeDtypeStruct((tiles * tile, columns), v.dtype)
    moved = (len(values) + 2) * tiles * tile * columns
    operands = (factor, *values, v)
    return run(kernel, (tiles,), [SMEM] + [at] * (len(values) + 1), own, shape, operands, moved)


def move_chunk(is_end, share, total, back, values, v, start, tiles, carried):
    columns, tile, count = v.shape[1], TILE * LINE, len(values)

    def kernel(is_end, total, back, v, *refs):
        values, (v_out, sq_out) = refs[:count], refs[-2:]
        moved = v[...] + jnp.where(is_end[0] > 0, back[...], total[...]) * share
        v_out[...] = moved

        @pl.when(pl.program_id(0) == 0)
        def _():
            sq_out[...] = refs[-3][...] if carried else jnp.zeros_like(sq_out)

        for i, value in enumerate(values):
            square = jnp.square(value[...] - moved)
            folded = sum(square[j : j + 8] for j in range(0, tile, 8))
            sq_out[i] += sum(folded[:, j : j + 128] for j in range(0, columns, 128))

    at, own = tiles_at(start, (tile, columns)), tiles_at(0, (tile, columns))
    squares = pl.BlockSpec((count, 8, 128), lambda i: (0, 0, 0))
    in_specs = [SMEM, own, own] + [at] * (count + 1)
    operands = (is_end, total, back, v, *values)
    aliases = {}
    if carried:
        in_specs += [pl.BlockSpec(memory_space=pl.ANY), squares]
        aliases = {len(operands): 0, len(operands) + 1: 1}
        operands += carried
    shapes = (
        jax.ShapeDtypeStruct(v.shape, v.dtype),
        jax.ShapeDtypeStruct((count, 8, 128), v.dtype),
    )
    moved = (count + 4) * tiles * tile * columns
    return run(kernel, (tiles,), in_specs, (at, squares), shapes, operands, moved, aliases)


def step_block(place, factor, values, v):
    _, rows, columns = v.shape
    parts = 4

    def kernel(place, factor, *refs):
        *values, v, out = refs
        out[...] = step_of(factor, values, v[...])

    at = pl.BlockSpec((None, rows, columns // parts), lambda i, place: (place[0], 0, i))
    own = pl.BlockSpec((rows, columns // parts), lambda i, place: (0, i))
    shape = jax.ShapeDtypeStruct((rows, columns), v.dtype)
    moved = (len(values) + 2) * rows * columns
    operands = (place, factor, *values, v)
    in_specs = [SMEM] + [at] * (len(values) + 1)
    return run(kernel, (parts,), in_specs, own, shape, operands, moved, prefetch=1)


def spread_only(mine, center, radius_total, worker_count):
    own_rows = center
    gathered = lax.all_to_all(mine, ("worker", "outer"), split_axis=0, concat_axis=0, tiled=True)
    for _ in range(ITERS):
        difference = gathered - own_rows[None]
        norm_sq = sum_over_devices(jnp.sum(difference * difference, axis=(1, 2)))
        factor = jnp.minimum(1.0, radius_total * lax.rsqrt(norm_sq + epsilon))
        own_rows = own_rows + jnp.sum(factor[:, None, None] * difference, axis=0) / worker_count
    return own_rows


def on_device(grads, center, radius):
    workers, outers = lax.axis_size("worker"), lax.axis_size("outer")
    worker_count = workers * outers
    radius_total = radius[0] * math.sqrt(D * KVW)
    rows, columns = center.shape
    mine = grads.reshape(worker_count, rows, columns)
    plan = split(rows, outers)
    if plan is None:
        return spread_only(mine, center, radius_total, worker_count)
    cut, sizes = plan
    rest = rows - cut

    w, o = lax.axis_index("worker"), lax.axis_index("outer")
    is_end = (o == 0) | (o == LINE - 1)
    is_low = o < LINE // 2

    def line_rows(source, worker):
        return lax.dynamic_slice(source, (worker * outers, cut, 0), (outers, rest, columns))

    tail = center[cut:]
    pair = send(tail, [(i, i ^ 1) for i in range(LINE)])
    steps = list(range(workers // 2, workers)) + list(range(1, workers // 2)) + [0]
    held, source = [], mine
    for step in steps:
        sent = line_rows(source, w ^ step)
        source = tie(source, sent)
        if step:
            swap = [(i, i ^ step) for i in range(workers)]
            sent = send(sent, swap, "worker")
        held.append(sent)
    spread = lax.all_to_all(
        mine[:, :cut], ("worker", "outer"), split_axis=0, concat_axis=0, tiled=True
    )
    first = (o % 2) == 0
    near = jnp.where(first, jnp.stack([tail, pair]), jnp.stack([pair, tail]))
    crossed = send(near, ACROSS)
    far = jnp.where(is_end, send(crossed, TO_ENDS), crossed)
    line_v = jnp.where(is_low, jnp.concatenate([near, far]), jnp.concatenate([far, near]))
    spread_v = center[:cut]

    places = jnp.stack([(w ^ step) * outers + o for step in steps])
    hit = places[:, None] == jnp.arange(worker_count)[None]

    def placed(line_sq):
        return jnp.sum(jnp.where(hit, line_sq[:, None], 0.0), axis=0)

    def factors(both):
        norm_sq = sum_over_devices(both)
        factor = jnp.minimum(1.0, radius_total * lax.rsqrt(norm_sq + epsilon))
        return factor, jnp.sum(jnp.where(hit, factor[None], 0.0), axis=1)

    def spread_norms(v):
        difference = spread - v[None]
        return jnp.sum(difference * difference, axis=(1, 2))

    def spread_update(v, factor):
        return v + jnp.sum(factor[:, None, None] * (spread - v[None]), axis=0) / worker_count

    line_sq, v = jnp.zeros((worker_count,), jnp.float32), line_v
    for place in reversed(range(workers)):
        square = jnp.sum(jnp.square(held[place] - v))
        line_sq = lax.optimization_barrier(line_sq + jnp.where(hit[place], square, 0.0))
        v = tie(v, line_sq)
    factor, line_factor = factors(spread_norms(spread_v) + line_sq)

    flat = [value.reshape(outers * rest, columns) for value in held]
    flat_v = line_v.reshape(outers * rest, columns)
    end_flag = is_end.astype(jnp.int32).reshape(1)
    start, carried, squares = 0, (), []
    for chunk, tiles in enumerate(sizes):
        own = step_chunk(line_factor, flat, flat_v, start, tiles)
        own = own + send(own, TO_MIDS)
        own = own + send(own, ACROSS)
        if chunk >= 3:
            own = tie(own, squares[chunk - 2])
        back = send(own, TO_ENDS)
        carried = tuple(
            move_chunk(end_flag, 1 / worker_count, own, back, flat, flat_v, start, tiles, carried)
        )
        squares.append(carried[1])
        start += tiles
    spread_v = spread_update(spread_v, factor)
    line_v = carried[0].reshape(line_v.shape)
    factor, line_factor = factors(spread_norms(spread_v) + placed(jnp.sum(carried[1], axis=(1, 2))))

    block, v = [], line_v
    for place in range(LINE):
        index = jnp.where(is_low, LINE - 1 - place, place).astype(jnp.int32).reshape(1)
        block.append(step_block(index, line_factor, held, v))
        v = tie(v, block[place])
    arrived = [send(block[place], TO_MIDS) for place in range(3)]
    passed = [send(block[place] + arrived[place], ACROSS) for place in range(2)]
    end_sum = block[3] + send(block[3] + passed[0], TO_ENDS)
    mid_sum = block[2] + arrived[2] + passed[1]
    own_v = lax.dynamic_index_in_dim(line_v, o, 0, keepdims=False)
    own_v = own_v + jnp.where(is_end, end_sum, mid_sum) / worker_count
    return jnp.concatenate([spread_update(spread_v, factor), own_v])


def solution(mesh):
    in_specs = (P("worker", "outer", None, "mp"), P(("worker", "outer"), "mp"), P())
    out_specs = P(("worker", "outer"), "mp")

    return jax.shard_map(on_device, mesh=mesh, in_specs=in_specs, out_specs=out_specs, check_vma=False)
```

```python
import math

import jax
import jax.numpy as jnp
from jax import lax
from jax.experimental import pallas as pl
from jax.experimental.pallas import tpu as pltpu
from jax.sharding import PartitionSpec as P


D = 3584
ITERS = 2
KVW = 4096
AXES = ("worker", "outer", "mp")
LINE = 4
TILE = 8
SPREAD = 0.4

epsilon = 1e-06


def sum_over_devices(value):
    for axis in AXES:
        size = lax.axis_size(axis)
        step = 1
        while step < size:
            value = value + lax.ppermute(value, axis, [(i, i ^ step) for i in range(size)])
            step *= 2
    return value


def send(value, pairs, axis="outer"):
    return lax.ppermute(value, axis, pairs)


TO_MIDS = [(0, 1), (3, 2)]
ACROSS = [(1, 2), (2, 1)]
TO_ENDS = [(1, 0), (2, 3)]


def tie(value, earlier):
    return lax.optimization_barrier((value, earlier))[0]


def split(rows, outers):
    cut = int(rows * SPREAD) // TILE * TILE
    rest = rows - cut
    if outers != LINE or rest % TILE or rest // TILE < 12:
        return None
    tiles = rest // TILE
    body = tiles - 6
    sizes = [1, 2] + [3] * (body // 3) + [body % 3] * (body % 3 > 0) + [1, 1, 1]
    return cut, sizes


SMEM = pl.BlockSpec(memory_space=pltpu.SMEM)


def tiles_at(start, shape):
    return pl.BlockSpec(shape, lambda i: (start + i, 0))


def run(kernel, grid, in_specs, out_specs, out_shape, operands, moved, aliases={}, prefetch=0):
    return pl.pallas_call(
        kernel,
        grid_spec=pltpu.PrefetchScalarGridSpec(
            num_scalar_prefetch=prefetch, grid=grid, in_specs=in_specs, out_specs=out_specs
        ),
        out_shape=out_shape,
        input_output_aliases=aliases,
        compiler_params=pltpu.CompilerParams(vmem_limit_bytes=60 << 20),
        cost_estimate=pl.CostEstimate(flops=4 * moved, bytes_accessed=4 * moved, transcendentals=0),
    )(*operands)


def step_of(factor, values, v):
    return sum(factor[i] * (value[...] - v) for i, value in enumerate(values))


def step_chunk(factor, values, v, start, tiles):
    columns, tile = v.shape[1], TILE * LINE

    def kernel(factor, *refs):
        *values, v, out = refs
        out[...] = step_of(factor, values, v[...])

    at, own = tiles_at(start, (tile, columns)), tiles_at(0, (tile, columns))
    shape = jax.ShapeDtypeStruct((tiles * tile, columns), v.dtype)
    moved = (len(values) + 2) * tiles * tile * columns
    operands = (factor, *values, v)
    return run(kernel, (tiles,), [SMEM] + [at] * (len(values) + 1), own, shape, operands, moved)


def move_chunk(is_end, share, total, back, values, v, start, tiles, carried):
    columns, tile, count = v.shape[1], TILE * LINE, len(values)

    def kernel(is_end, total, back, v, *refs):
        values, (v_out, sq_out) = refs[:count], refs[-2:]
        moved = v[...] + jnp.where(is_end[0] > 0, back[...], total[...]) * share
        v_out[...] = moved

        @pl.when(pl.program_id(0) == 0)
        def _():
            sq_out[...] = refs[-3][...] if carried else jnp.zeros_like(sq_out)

        for i, value in enumerate(values):
            square = jnp.square(value[...] - moved)
            folded = sum(square[j : j + 8] for j in range(0, tile, 8))
            sq_out[i] += sum(folded[:, j : j + 128] for j in range(0, columns, 128))

    at, own = tiles_at(start, (tile, columns)), tiles_at(0, (tile, columns))
    squares = pl.BlockSpec((count, 8, 128), lambda i: (0, 0, 0))
    in_specs = [SMEM, own, own] + [at] * (count + 1)
    operands = (is_end, total, back, v, *values)
    aliases = {}
    if carried:
        in_specs += [pl.BlockSpec(memory_space=pl.ANY), squares]
        aliases = {len(operands): 0, len(operands) + 1: 1}
        operands += carried
    shapes = (
        jax.ShapeDtypeStruct(v.shape, v.dtype),
        jax.ShapeDtypeStruct((count, 8, 128), v.dtype),
    )
    moved = (count + 4) * tiles * tile * columns
    return run(kernel, (tiles,), in_specs, (at, squares), shapes, operands, moved, aliases)


def step_block(place, factor, values, v):
    _, rows, columns = v.shape
    parts = 4

    def kernel(place, factor, *refs):
        *values, v, out = refs
        out[...] = step_of(factor, values, v[...])

    at = pl.BlockSpec((None, rows, columns // parts), lambda i, place: (place[0], 0, i))
    own = pl.BlockSpec((rows, columns // parts), lambda i, place: (0, i))
    shape = jax.ShapeDtypeStruct((rows, columns), v.dtype)
    moved = (len(values) + 2) * rows * columns
    operands = (place, factor, *values, v)
    in_specs = [SMEM] + [at] * (len(values) + 1)
    return run(kernel, (parts,), in_specs, own, shape, operands, moved, prefetch=1)


def spread_only(mine, center, radius_total, worker_count):
    own_rows = center
    gathered = lax.all_to_all(mine, ("worker", "outer"), split_axis=0, concat_axis=0, tiled=True)
    for _ in range(ITERS):
        difference = gathered - own_rows[None]
        norm_sq = sum_over_devices(jnp.sum(difference * difference, axis=(1, 2)))
        factor = jnp.minimum(1.0, radius_total * lax.rsqrt(norm_sq + epsilon))
        own_rows = own_rows + jnp.sum(factor[:, None, None] * difference, axis=0) / worker_count
    return own_rows


def on_device(grads, center, radius):
    workers, outers = lax.axis_size("worker"), lax.axis_size("outer")
    worker_count = workers * outers
    radius_total = radius[0] * math.sqrt(D * KVW)
    rows, columns = center.shape
    mine = grads.reshape(worker_count, rows, columns)
    plan = split(rows, outers)
    if plan is None:
        return spread_only(mine, center, radius_total, worker_count)
    cut, sizes = plan
    rest = rows - cut

    w, o = lax.axis_index("worker"), lax.axis_index("outer")
    is_end = (o == 0) | (o == LINE - 1)
    is_low = o < LINE // 2

    def line_rows(source, worker):
        return lax.dynamic_slice(source, (worker * outers, cut, 0), (outers, rest, columns))

    tail = center[cut:]
    pair = send(tail, [(i, i ^ 1) for i in range(LINE)])
    steps = list(range(workers // 2, workers)) + list(range(1, workers // 2)) + [0]
    held, source = [], mine
    for step in steps:
        sent = line_rows(source, w ^ step)
        source = tie(source, sent)
        if step:
            swap = [(i, i ^ step) for i in range(workers)]
            sent = send(sent, swap, "worker")
        held.append(sent)
    spread = lax.all_to_all(
        mine[:, :cut], ("worker", "outer"), split_axis=0, concat_axis=0, tiled=True
    )
    first = (o % 2) == 0
    near = jnp.where(first, jnp.stack([tail, pair]), jnp.stack([pair, tail]))
    crossed = send(near, ACROSS)
    far = jnp.where(is_end, send(crossed, TO_ENDS), crossed)
    line_v = jnp.where(is_low, jnp.concatenate([near, far]), jnp.concatenate([far, near]))
    spread_v = center[:cut]

    places = jnp.stack([(w ^ step) * outers + o for step in steps])
    hit = places[:, None] == jnp.arange(worker_count)[None]

    def placed(line_sq):
        return jnp.sum(jnp.where(hit, line_sq[:, None], 0.0), axis=0)

    def factors(both):
        norm_sq = sum_over_devices(both)
        factor = jnp.minimum(1.0, radius_total * lax.rsqrt(norm_sq + epsilon))
        return factor, jnp.sum(jnp.where(hit, factor[None], 0.0), axis=1)

    def spread_norms(v):
        difference = spread - v[None]
        return jnp.sum(difference * difference, axis=(1, 2))

    def spread_update(v, factor):
        return v + jnp.sum(factor[:, None, None] * (spread - v[None]), axis=0) / worker_count

    line_sq, v = jnp.zeros((worker_count,), jnp.float32), line_v
    for place in reversed(range(workers)):
        square = jnp.sum(jnp.square(held[place] - v))
        line_sq = lax.optimization_barrier(line_sq + jnp.where(hit[place], square, 0.0))
        v = tie(v, line_sq)
    factor, line_factor = factors(spread_norms(spread_v) + line_sq)

    flat = [value.reshape(outers * rest, columns) for value in held]
    flat_v = line_v.reshape(outers * rest, columns)
    end_flag = is_end.astype(jnp.int32).reshape(1)
    start, carried, squares, totals = 0, (), [], []
    next_spread_v = spread_update(spread_v, factor)
    spread_sq = spread_norms(next_spread_v)
    early = {1: next_spread_v, 2: spread_sq}
    for chunk, tiles in enumerate(sizes):
        own = step_chunk(line_factor, flat, flat_v, start, tiles)
        got = send(own, TO_MIDS)
        if chunk >= 2:
            got = tie(got, totals[chunk - 2])
        own = own + got
        own = own + send(own, ACROSS)
        if chunk in early:
            own = tie(own, early[chunk])
        if chunk >= 3:
            own = tie(own, squares[chunk - 3])
        totals.append(own)
        back = send(own, TO_ENDS)
        carried = tuple(
            move_chunk(end_flag, 1 / worker_count, own, back, flat, flat_v, start, tiles, carried)
        )
        squares.append(carried[1])
        start += tiles
    spread_v = next_spread_v
    line_v = carried[0].reshape(line_v.shape)
    factor, line_factor = factors(spread_sq + placed(jnp.sum(carried[1], axis=(1, 2))))

    block, v = [], line_v
    for place in range(LINE):
        index = jnp.where(is_low, LINE - 1 - place, place).astype(jnp.int32).reshape(1)
        block.append(step_block(index, line_factor, held, v))
        v = tie(v, block[place])
    arrived = [send(block[place], TO_MIDS) for place in range(3)]
    passed = [send(block[place] + arrived[place], ACROSS) for place in range(2)]
    end_sum = block[3] + send(block[3] + passed[0], TO_ENDS)
    mid_sum = block[2] + arrived[2] + passed[1]
    own_v = lax.dynamic_index_in_dim(line_v, o, 0, keepdims=False)
    own_v = own_v + jnp.where(is_end, end_sum, mid_sum) / worker_count
    return jnp.concatenate([spread_update(spread_v, factor), own_v])


def solution(mesh):
    in_specs = (P("worker", "outer", None, "mp"), P(("worker", "outer"), "mp"), P())
    out_specs = P(("worker", "outer"), "mp")

    return jax.shard_map(on_device, mesh=mesh, in_specs=in_specs, out_specs=out_specs, check_vma=False)
```

```python
import math

import jax
import jax.numpy as jnp
from jax import lax
from jax.experimental import pallas as pl
from jax.experimental.pallas import tpu as pltpu
from jax.sharding import PartitionSpec as P


D = 3584
ITERS = 2
KVW = 4096
AXES = ("worker", "outer", "mp")
LINE = 4
TILE = 8
SPREAD = 3 / 7
AHEAD = 16

epsilon = 1e-06


def sum_over_devices(value):
    for axis in AXES:
        size = lax.axis_size(axis)
        step = 1
        while step < size:
            value = value + lax.ppermute(value, axis, [(i, i ^ step) for i in range(size)])
            step *= 2
    return value


def send(value, pairs, axis="outer"):
    return lax.ppermute(value, axis, pairs)


TO_MIDS = [(0, 1), (3, 2)]
ACROSS = [(1, 2), (2, 1)]
TO_ENDS = [(1, 0), (2, 3)]


def tie(value, earlier):
    return lax.optimization_barrier((value, earlier))[0]


def split(rows, outers):
    cut = int(rows * SPREAD) // TILE * TILE
    rest = rows - cut
    tiles = rest // TILE
    if outers != LINE or rest % TILE or tiles < 10 or cut <= AHEAD:
        return None
    body = tiles - 7
    sizes = [1, 2] + [3] * (body // 3) + [body % 3] * (body % 3 > 0) + [2, 1, 1]
    return cut, sizes


SMEM = pl.BlockSpec(memory_space=pltpu.SMEM)


def run(kernel, grid, in_specs, out_specs, out_shape, operands, moved, aliases={}, prefetch=0):
    return pl.pallas_call(
        kernel,
        grid_spec=pltpu.PrefetchScalarGridSpec(
            num_scalar_prefetch=prefetch, grid=grid, in_specs=in_specs, out_specs=out_specs
        ),
        out_shape=out_shape,
        input_output_aliases=aliases,
        compiler_params=pltpu.CompilerParams(vmem_limit_bytes=60 << 20),
        cost_estimate=pl.CostEstimate(flops=4 * moved, bytes_accessed=4 * moved, transcendentals=0),
    )(*operands)


def group_spec(begin, count, tile, columns):
    return pl.BlockSpec((tile, columns), lambda i: (jnp.clip(i - begin, 0, count - 1), 0))


def begins(sizes):
    return [sum(sizes[:i]) for i in range(len(sizes))]


def step_of(factor, values, v):
    return sum(factor[i] * (value[...] - v) for i, value in enumerate(values))


def step_chunks(factor, values, v, start, sizes):
    columns, tile, count = v.shape[1], TILE * LINE, len(values)
    places = begins(sizes)

    def kernel(factor, *refs):
        values, v, outs = refs[:count], refs[count], refs[count + 1 :]
        i = pl.program_id(0)
        total = step_of(factor, values, v[...])
        for out, begin, size in zip(outs, places, sizes):

            @pl.when((i >= begin) & (i < begin + size))
            def _(out=out):
                out[...] = total

    at = pl.BlockSpec((tile, columns), lambda i: (start + i, 0))
    outs = [group_spec(begin, size, tile, columns) for begin, size in zip(places, sizes)]
    shapes = [jax.ShapeDtypeStruct((size * tile, columns), v.dtype) for size in sizes]
    moved = (count + 2) * sum(sizes) * tile * columns
    in_specs = [SMEM] + [at] * (count + 1)
    return run(kernel, (sum(sizes),), in_specs, outs, shapes, (factor, *values, v), moved)


def move_chunks(is_end, share, totals, backs, values, v, start, sizes, carried):
    columns, tile, count, chunks = v.shape[1], TILE * LINE, len(values), len(sizes)
    places = begins(sizes)

    def kernel(is_end, v, *refs):
        values, rest = refs[:count], refs[count:]
        totals, backs, (v_out, sq_out) = rest[:chunks], rest[chunks : 2 * chunks], rest[-2:]
        i = pl.program_id(0)

        @pl.when(i == 0)
        def _():
            sq_out[...] = rest[-3][...] if carried else jnp.zeros_like(sq_out)

        for total, back, begin, size in zip(totals, backs, places, sizes):

            @pl.when((i >= begin) & (i < begin + size))
            def _(total=total, back=back):
                step = jnp.where(is_end[0] > 0, back[...], total[...])
                v_out[...] = v[...] + step * share

        moved = v_out[...]
        for k, value in enumerate(values):
            square = jnp.square(value[...] - moved)
            folded = sum(square[j : j + 8] for j in range(0, tile, 8))
            sq_out[k] += sum(folded[:, j : j + 128] for j in range(0, columns, 128))

    at = pl.BlockSpec((tile, columns), lambda i: (start + i, 0))
    squares = pl.BlockSpec((count, 8, 128), lambda i: (0, 0, 0))
    parts = [group_spec(begin, size, tile, columns) for begin, size in zip(places, sizes)]
    in_specs = [SMEM] + [at] * (count + 1) + parts + parts
    operands = (is_end, v, *values, *totals, *backs)
    aliases = {}
    if carried:
        in_specs += [pl.BlockSpec(memory_space=pl.ANY), squares]
        aliases = {len(operands): 0, len(operands) + 1: 1}
        operands += tuple(carried)
    shapes = (
        jax.ShapeDtypeStruct(v.shape, v.dtype),
        jax.ShapeDtypeStruct((count, 8, 128), v.dtype),
    )
    moved = (count + 4) * sum(sizes) * tile * columns
    return run(kernel, (sum(sizes),), in_specs, (at, squares), shapes, operands, moved, aliases)


def step_blocks(places, factor, values, v, rest):
    columns, count, blocks = v.shape[1], len(values), len(places)
    tile = TILE * LINE if rest % (TILE * LINE) == 0 else TILE
    size = rest // tile

    def kernel(places, factor, *refs):
        values, v, outs = refs[:count], refs[count], refs[count + 1 :]
        i = pl.program_id(0)
        total = step_of(factor, values, v[...])
        for k, out in enumerate(outs):

            @pl.when(i // size == k)
            def _(out=out):
                out[...] = total

    at = pl.BlockSpec((tile, columns), lambda i, places: (places[i // size] * size + i % size, 0))
    outs = [
        pl.BlockSpec((tile, columns), lambda i, _, k=k: (jnp.clip(i - k * size, 0, size - 1), 0))
        for k in range(blocks)
    ]
    shapes = [jax.ShapeDtypeStruct((rest, columns), v.dtype)] * blocks
    moved = (count + 2) * blocks * rest * columns
    operands = (jnp.stack(places).astype(jnp.int32), factor, *values, v)
    in_specs = [SMEM] + [at] * (count + 1)
    return run(kernel, (blocks * size,), in_specs, outs, shapes, operands, moved, prefetch=1)


def spread_only(mine, center, radius_total, worker_count):
    own_rows = center
    gathered = lax.all_to_all(mine, ("worker", "outer"), split_axis=0, concat_axis=0, tiled=True)
    for _ in range(ITERS):
        difference = gathered - own_rows[None]
        norm_sq = sum_over_devices(jnp.sum(difference * difference, axis=(1, 2)))
        factor = jnp.minimum(1.0, radius_total * lax.rsqrt(norm_sq + epsilon))
        own_rows = own_rows + jnp.sum(factor[:, None, None] * difference, axis=0) / worker_count
    return own_rows


def on_device(grads, center, radius):
    workers, outers = lax.axis_size("worker"), lax.axis_size("outer")
    worker_count = workers * outers
    radius_total = radius[0] * math.sqrt(D * KVW)
    rows, columns = center.shape
    mine = grads.reshape(worker_count, rows, columns)
    plan = split(rows, outers)
    if plan is None:
        return spread_only(mine, center, radius_total, worker_count)
    cut, sizes = plan
    rest = rows - cut

    w, o = lax.axis_index("worker"), lax.axis_index("outer")
    is_end = (o == 0) | (o == LINE - 1)
    is_low = o < LINE // 2

    def line_rows(source, worker):
        return lax.dynamic_slice(source, (worker * outers, cut, 0), (outers, rest, columns))

    tail = center[cut:]
    pair = send(tail, [(i, i ^ 1) for i in range(LINE)])
    steps = list(range(workers // 2, workers)) + list(range(1, workers // 2)) + [0]
    held, source = [], mine
    for step in steps:
        sent = line_rows(source, w ^ step)
        source = tie(source, sent)
        if step:
            swap = [(i, i ^ step) for i in range(workers)]
            sent = send(sent, swap, "worker")
        held.append(sent)
    edges = [(0, AHEAD), (AHEAD, cut)]
    spread = []
    for low, high in edges:
        spread.append(
            lax.all_to_all(
                mine[:, low:high], ("worker", "outer"), split_axis=0, concat_axis=0, tiled=True
            )
        )
    first = (o % 2) == 0
    near = jnp.where(first, jnp.stack([tail, pair]), jnp.stack([pair, tail]))
    crossed = send(near, ACROSS)
    far = jnp.where(is_end, send(crossed, TO_ENDS), crossed)
    line_v = jnp.where(is_low, jnp.concatenate([near, far]), jnp.concatenate([far, near]))
    spread_v = [center[low:high] for low, high in edges]

    places = jnp.stack([(w ^ step) * outers + o for step in steps])
    hit = places[:, None] == jnp.arange(worker_count)[None]

    def placed(line_sq):
        return jnp.sum(jnp.where(hit, line_sq[:, None], 0.0), axis=0)

    def factors(both):
        norm_sq = sum_over_devices(both)
        factor = jnp.minimum(1.0, radius_total * lax.rsqrt(norm_sq + epsilon))
        return factor, jnp.sum(jnp.where(hit, factor[None], 0.0), axis=1)

    def spread_norms(values):
        return [
            jnp.sum(jnp.square(part - v[None]), axis=(1, 2)) for part, v in zip(spread, values)
        ]

    def spread_update(values, factor):
        weight = factor[:, None, None]
        return [
            v + jnp.sum(weight * (part - v[None]), axis=0) / worker_count
            for part, v in zip(spread, values)
        ]

    line_sq, v = jnp.zeros((worker_count,), jnp.float32), line_v
    for place in reversed(range(workers)):
        square = jnp.sum(jnp.square(held[place] - v))
        line_sq = lax.optimization_barrier(line_sq + jnp.where(hit[place], square, 0.0))
        v = tie(v, line_sq)
    ahead, last = spread_norms(spread_v)
    factor, line_factor = factors(last + lax.optimization_barrier(line_sq + ahead))

    flat = [value.reshape(outers * rest, columns) for value in held]
    flat_v = line_v.reshape(outers * rest, columns)
    end_flag = is_end.astype(jnp.int32).reshape(1)
    next_spread_v = spread_update(spread_v, factor)
    spread_sq = sum(spread_norms(next_spread_v))
    early = {1: next_spread_v, 2: spread_sq}
    count, places = len(sizes), begins(sizes)
    own = step_chunks(line_factor, flat, flat_v, 0, sizes[:2])
    own += step_chunks(line_factor, flat, tie(flat_v, own[0]), places[2], sizes[2:])
    groups = [slice(0, count - 5), slice(count - 5, count - 2), slice(count - 2, count)]
    totals, backs, carried = [], [], ()

    def move(part, carried):
        return move_chunks(
            end_flag, 1 / worker_count, totals[part], backs[part], flat, flat_v,
            places[part.start], sizes[part], carried,
        )

    for chunk in range(count):
        got = send(own[chunk], TO_MIDS)
        if chunk >= 2:
            got = tie(got, totals[chunk - 2])
        total = own[chunk] + got
        total = total + send(total, ACROSS)
        if chunk in early:
            total = tie(total, early[chunk])
        if chunk == count - 2:
            carried = move(groups[0], carried)
            total = tie(total, carried[1])
        totals.append(total)
        backs.append(send(total, TO_ENDS))
    for part in groups[1:]:
        carried = move(part, carried)
    spread_v = next_spread_v
    flat_v = carried[0]
    line_v = flat_v.reshape(line_v.shape)
    factor, line_factor = factors(spread_sq + placed(jnp.sum(carried[1], axis=(1, 2))))

    order = [jnp.where(is_low, LINE - 1 - place, place) for place in range(LINE)]
    block = step_blocks(order[:1], line_factor, flat, flat_v, rest)
    block += step_blocks(order[1:], line_factor, flat, tie(flat_v, block[0]), rest)
    arrived = [send(block[place], TO_MIDS) for place in range(3)]
    passed = [send(block[place] + arrived[place], ACROSS) for place in range(2)]
    end_sum = block[3] + send(block[3] + passed[0], TO_ENDS)
    mid_sum = block[2] + arrived[2] + passed[1]
    own_v = lax.dynamic_index_in_dim(line_v, o, 0, keepdims=False)
    own_v = own_v + jnp.where(is_end, end_sum, mid_sum) / worker_count
    return jnp.concatenate([*spread_update(spread_v, factor), own_v])


def solution(mesh):
    in_specs = (P("worker", "outer", None, "mp"), P(("worker", "outer"), "mp"), P())
    out_specs = P(("worker", "outer"), "mp")

    return jax.shard_map(on_device, mesh=mesh, in_specs=in_specs, out_specs=out_specs, check_vma=False)
```

```python
import math

import jax
import jax.numpy as jnp
from jax import lax
from jax.experimental import pallas as pl
from jax.experimental.pallas import tpu as pltpu
from jax.sharding import PartitionSpec as P


D = 3584
ITERS = 2
KVW = 4096
AXES = ("worker", "outer", "mp")
LINE = 4
TILE = 8
SPREAD = 3 / 7

epsilon = 1e-06


def sum_over_devices(value):
    for axis in AXES:
        size = lax.axis_size(axis)
        step = 1
        while step < size:
            value = value + lax.ppermute(value, axis, [(i, i ^ step) for i in range(size)])
            step *= 2
    return value


def send(value, pairs, axis="outer"):
    return lax.ppermute(value, axis, pairs)


TO_MIDS = [(0, 1), (3, 2)]
ACROSS = [(1, 2), (2, 1)]
TO_ENDS = [(1, 0), (2, 3)]


def tie(value, earlier):
    return lax.optimization_barrier((value, earlier))[0]


def split(rows, outers):
    cut = int(rows * SPREAD) // TILE * TILE
    rest = rows - cut
    tiles = rest // TILE
    if outers != LINE or rest % TILE or cut % TILE or tiles < 13 or not cut:
        return None
    body = tiles - 10
    sizes = [1, 2] + [3] * (body // 3) + [body % 3] * (body % 3 > 0) + [2, 2, 1, 1, 1]
    return cut, sizes


def hops(workers, outers):
    near, far = range(workers // 2), range(workers // 2, workers)
    wide = range(outers // 2, outers)
    first = [(far[0], 0)]
    second = [(0, j) for j in wide]
    third = [(k, j) for k in near[1:] for j in wide] + [(k, j) for k in far for j in wide]
    third += [(k, 0) for k in far[1:]] + [(k, 0) for k in near[1:]]
    fourth = [(k, j) for k in range(workers) for j in range(1, outers // 2)]
    return first, second, third, fourth


SMEM = pl.BlockSpec(memory_space=pltpu.SMEM)


def run(kernel, grid, in_specs, out_specs, out_shape, operands, moved, aliases={}, prefetch=0):
    return pl.pallas_call(
        kernel,
        grid_spec=pltpu.PrefetchScalarGridSpec(
            num_scalar_prefetch=prefetch, grid=grid, in_specs=in_specs, out_specs=out_specs
        ),
        out_shape=out_shape,
        input_output_aliases=aliases,
        compiler_params=pltpu.CompilerParams(vmem_limit_bytes=60 << 20),
        cost_estimate=pl.CostEstimate(flops=4 * moved, bytes_accessed=4 * moved, transcendentals=0),
    )(*operands)


def group_spec(begin, count, tile, columns):
    return pl.BlockSpec((tile, columns), lambda i: (jnp.clip(i - begin, 0, count - 1), 0))


def begins(sizes):
    return [sum(sizes[:i]) for i in range(len(sizes))]


def step_of(factor, values, v):
    return sum(factor[i] * (value[...] - v) for i, value in enumerate(values))


def step_chunks(factor, values, v, start, sizes):
    columns, tile, count = v.shape[1], TILE * LINE, len(values)
    places = begins(sizes)

    def kernel(factor, *refs):
        values, v, outs = refs[:count], refs[count], refs[count + 1 :]
        i = pl.program_id(0)
        total = step_of(factor, values, v[...])
        for out, begin, size in zip(outs, places, sizes):

            @pl.when((i >= begin) & (i < begin + size))
            def _(out=out):
                out[...] = total

    at = pl.BlockSpec((tile, columns), lambda i: (start + i, 0))
    outs = [group_spec(begin, size, tile, columns) for begin, size in zip(places, sizes)]
    shapes = [jax.ShapeDtypeStruct((size * tile, columns), v.dtype) for size in sizes]
    moved = (count + 2) * sum(sizes) * tile * columns
    in_specs = [SMEM] + [at] * (count + 1)
    return run(kernel, (sum(sizes),), in_specs, outs, shapes, (factor, *values, v), moved)


def move_chunks(is_end, share, totals, backs, values, v, start, sizes, carried):
    columns, tile, count, chunks = v.shape[1], TILE * LINE, len(values), len(sizes)
    places = begins(sizes)

    def kernel(is_end, v, *refs):
        values, rest = refs[:count], refs[count:]
        totals, backs, (v_out, sq_out) = rest[:chunks], rest[chunks : 2 * chunks], rest[-2:]
        i = pl.program_id(0)

        @pl.when(i == 0)
        def _():
            sq_out[...] = rest[-3][...] if carried else jnp.zeros_like(sq_out)

        for total, back, begin, size in zip(totals, backs, places, sizes):

            @pl.when((i >= begin) & (i < begin + size))
            def _(total=total, back=back):
                step = jnp.where(is_end[0] > 0, back[...], total[...])
                v_out[...] = v[...] + step * share

        moved = v_out[...]
        for k, value in enumerate(values):
            square = jnp.square(value[...] - moved)
            folded = sum(square[j : j + 8] for j in range(0, tile, 8))
            sq_out[k] += sum(folded[:, j : j + 128] for j in range(0, columns, 128))

    at = pl.BlockSpec((tile, columns), lambda i: (start + i, 0))
    squares = pl.BlockSpec((count, 8, 128), lambda i: (0, 0, 0))
    parts = [group_spec(begin, size, tile, columns) for begin, size in zip(places, sizes)]
    in_specs = [SMEM] + [at] * (count + 1) + parts + parts
    operands = (is_end, v, *values, *totals, *backs)
    aliases = {}
    if carried:
        in_specs += [pl.BlockSpec(memory_space=pl.ANY), squares]
        aliases = {len(operands): 0, len(operands) + 1: 1}
        operands += tuple(carried)
    shapes = (
        jax.ShapeDtypeStruct(v.shape, v.dtype),
        jax.ShapeDtypeStruct((count, 8, 128), v.dtype),
    )
    moved = (count + 4) * sum(sizes) * tile * columns
    return run(kernel, (sum(sizes),), in_specs, (at, squares), shapes, operands, moved, aliases)


def step_blocks(places, factor, values, v, rest):
    columns, count, blocks = v.shape[1], len(values), len(places)
    tile = TILE * LINE if rest % (TILE * LINE) == 0 else TILE
    size = rest // tile

    def kernel(places, factor, *refs):
        values, v, outs = refs[:count], refs[count], refs[count + 1 :]
        i = pl.program_id(0)
        total = step_of(factor, values, v[...])
        for k, out in enumerate(outs):

            @pl.when(i // size == k)
            def _(out=out):
                out[...] = total

    at = pl.BlockSpec((tile, columns), lambda i, places: (places[i // size] * size + i % size, 0))
    outs = [
        pl.BlockSpec((tile, columns), lambda i, _, k=k: (jnp.clip(i - k * size, 0, size - 1), 0))
        for k in range(blocks)
    ]
    shapes = [jax.ShapeDtypeStruct((rest, columns), v.dtype)] * blocks
    moved = (count + 2) * blocks * rest * columns
    operands = (jnp.stack(places).astype(jnp.int32), factor, *values, v)
    in_specs = [SMEM] + [at] * (count + 1)
    return run(kernel, (blocks * size,), in_specs, outs, shapes, operands, moved, prefetch=1)


def row_tile(rows):
    return next(tile for tile in (32, 16, 8) if rows % tile == 0)


def move_spread(share, factor, values, v):
    (rows, columns), count = v.shape, len(values)
    tile = row_tile(rows)

    def kernel(factor, v, *refs):
        values, (v_out, sq_out) = refs[:count], refs[-2:]
        moved = v[...] + step_of(factor, values, v[...]) * share
        v_out[...] = moved

        @pl.when(pl.program_id(0) == 0)
        def _():
            sq_out[...] = jnp.zeros_like(sq_out)

        for k, value in enumerate(values):
            square = jnp.square(value[...] - moved)
            folded = sum(square[j : j + 8] for j in range(0, tile, 8))
            sq_out[k] += sum(folded[:, j : j + 128] for j in range(0, columns, 128))

    at = pl.BlockSpec((tile, columns), lambda i: (i, 0))
    squares = pl.BlockSpec((count, 8, 128), lambda i: (0, 0, 0))
    shapes = (
        jax.ShapeDtypeStruct(v.shape, v.dtype),
        jax.ShapeDtypeStruct((count, 8, 128), v.dtype),
    )
    in_specs, moved = [SMEM] + [at] * (count + 1), (count + 2) * rows * columns
    return run(kernel, (rows // tile,), in_specs, (at, squares), shapes, (factor, v, *values), moved)


def end_spread(share, factor, values, v, rows):
    (cut, columns), count = v.shape, len(values)
    tile = row_tile(cut)

    def kernel(factor, v, *refs):
        refs[-1][...] = v[...] + step_of(factor, refs[:count], v[...]) * share

    at = pl.BlockSpec((tile, columns), lambda i: (i, 0))
    shape = jax.ShapeDtypeStruct((rows, columns), v.dtype)
    in_specs, moved = [SMEM] + [at] * (count + 1), (count + 2) * cut * columns
    return run(kernel, (cut // tile,), in_specs, at, shape, (factor, v, *values), moved)


def end_line(share, place, is_end, v, end_parts, mid_parts, buffer, cut):
    rows, columns = end_parts[0].shape
    tile = row_tile(math.gcd(rows, cut))
    ends = len(end_parts)
    offset, size = cut // tile, rows // tile

    def kernel(place, is_end, v, *refs):
        parts, out = refs[:-2], refs[-1]
        end = sum(part[...] for part in parts[:ends])
        mid = sum(part[...] for part in parts[ends:])
        out[...] = v[...] + jnp.where(is_end[0] > 0, end, mid) * share

    at = pl.BlockSpec((tile, columns), lambda i, place: (i, 0))
    own = pl.BlockSpec((tile, columns), lambda i, place: (place[0] * size + i, 0))
    out = pl.BlockSpec((tile, columns), lambda i, place: (offset + i, 0))
    operands = (place, is_end, v, *end_parts, *mid_parts, buffer)
    in_specs = [SMEM, own] + [at] * (len(operands) - 4) + [pl.BlockSpec(memory_space=pl.ANY)]
    shape = jax.ShapeDtypeStruct(buffer.shape, buffer.dtype)
    aliases = {len(operands) - 1: 0}
    moved = (len(operands) - 2) * rows * columns
    return run(kernel, (size,), in_specs, out, shape, operands, moved, aliases, prefetch=1)


def spread_only(mine, center, radius_total, worker_count):
    own_rows = center
    gathered = lax.all_to_all(mine, ("worker", "outer"), split_axis=0, concat_axis=0, tiled=True)
    for _ in range(ITERS):
        difference = gathered - own_rows[None]
        norm_sq = sum_over_devices(jnp.sum(difference * difference, axis=(1, 2)))
        factor = jnp.minimum(1.0, radius_total * lax.rsqrt(norm_sq + epsilon))
        own_rows = own_rows + jnp.sum(factor[:, None, None] * difference, axis=0) / worker_count
    return own_rows


def on_device(grads, center, radius):
    workers, outers = lax.axis_size("worker"), lax.axis_size("outer")
    worker_count = workers * outers
    radius_total = radius[0] * math.sqrt(D * KVW)
    rows, columns = center.shape
    mine = grads.reshape(worker_count, rows, columns)
    plan = split(rows, outers)
    if plan is None:
        return spread_only(mine, center, radius_total, worker_count)
    cut, sizes = plan
    rest = rows - cut

    w, o = lax.axis_index("worker"), lax.axis_index("outer")
    is_end = (o == 0) | (o == LINE - 1)
    is_low = o < LINE // 2

    source = [mine]

    def take(step, turn, low, count, size):
        begin = (w ^ step) * outers + (o ^ turn if count == 1 else 0)
        rows_out = lax.dynamic_slice(source[0], (begin, low, 0), (count, size, columns))
        if not (step or turn):
            return rows_out
        source[0] = tie(source[0], rows_out)
        jump = step * outers + turn
        pairs = [(i, i ^ jump) for i in range(worker_count)]
        return send(rows_out, pairs, ("worker", "outer"))

    tail = center[cut:]
    flows = hops(workers, outers)
    spread = {(0, 0): take(0, 0, 0, 1, cut)}
    held = {0: take(0, 0, cut, outers, rest)}
    far, near = list(range(workers // 2, workers)), list(range(1, workers // 2))
    for flow in flows[0]:
        spread[flow] = take(*flow, 0, 1, cut)
    pair = send(tail, [(i, i ^ 1) for i in range(LINE)])
    held[far[0]] = take(far[0], 0, cut, outers, rest)
    for flow in flows[1]:
        spread[flow] = take(*flow, 0, 1, cut)
    for step in far[1:]:
        held[step] = take(step, 0, cut, outers, rest)
    for flow in flows[2]:
        spread[flow] = take(*flow, 0, 1, cut)
    for step in near:
        held[step] = take(step, 0, cut, outers, rest)
    for flow in flows[3]:
        spread[flow] = take(*flow, 0, 1, cut)
    first = (o % 2) == 0
    side = jnp.where(first, jnp.stack([tail, pair]), jnp.stack([pair, tail]))
    crossed = send(side, ACROSS)
    other = jnp.where(is_end, send(crossed, TO_ENDS), crossed)
    line_v = jnp.where(is_low, jnp.concatenate([side, other]), jnp.concatenate([other, side]))
    spread_v, share = center[:cut], 1 / worker_count
    numbers = jnp.arange(worker_count)
    steps = [0] + near + far
    hit = jnp.stack([(w ^ step) * outers + o for step in steps])[:, None] == numbers[None]
    turns = [(step, turn) for step in range(workers) for turn in range(outers)]
    spots = jnp.stack([(w ^ step) * outers + (o ^ turn) for step, turn in turns])
    spread_hit = spots[:, None] == numbers[None]

    def placed(line_sq, hit):
        return jnp.sum(jnp.where(hit, line_sq[:, None], 0.0), axis=0)

    def factors(both):
        norm_sq = sum_over_devices(both)
        factor = jnp.minimum(1.0, radius_total * lax.rsqrt(norm_sq + epsilon))
        return [jnp.sum(jnp.where(at, factor[None], 0.0), axis=1) for at in (spread_hit, hit)]

    early = [(0, 0)] + flows[0] + flows[1] + [f for f in flows[2] if f[0] < workers // 2]
    early += [f for f in flows[3] if f[0] < workers // 2]
    late = [f for f in flows[2] if f[0] >= workers // 2] + [f for f in flows[3] if f[0] >= workers // 2]
    norms = jnp.zeros((worker_count,), jnp.float32)

    def add_norm(norms, value, base, spot):
        square = jnp.sum(jnp.square(value - base))
        return lax.optimization_barrier(norms + jnp.where(numbers == spot, square, 0.0))

    for step, turn in early:
        norms = add_norm(norms, spread[step, turn][0], tie(spread_v, norms), (w ^ step) * outers + (o ^ turn))
    for step in steps:
        norms = add_norm(norms, held[step], tie(line_v, norms), (w ^ step) * outers + o)
    for step, turn in late:
        norms = add_norm(norms, spread[step, turn][0], tie(spread_v, norms), (w ^ step) * outers + (o ^ turn))
    factor, line_factor = factors(norms)

    spread = [spread[turn].reshape(cut, columns) for turn in turns]
    flat = [held[step].reshape(outers * rest, columns) for step in steps]
    flat_v = line_v.reshape(outers * rest, columns)
    end_flag = is_end.astype(jnp.int32).reshape(1)
    next_spread_v, spread_sq = move_spread(share, factor, spread, spread_v)
    early = {1: next_spread_v}
    count, places = len(sizes), begins(sizes)
    own = step_chunks(line_factor, flat, flat_v, 0, sizes[:1])
    own += step_chunks(line_factor, flat, tie(flat_v, own[0]), places[1], sizes[1:2])
    own += step_chunks(line_factor, flat, tie(flat_v, own[1]), places[2], sizes[2:])
    groups = [slice(0, count - 5), slice(count - 5, count - 2), slice(count - 2, count)]
    totals, backs, carried = [], [], ()

    def move(part, carried):
        return move_chunks(
            end_flag, share, totals[part], backs[part], flat, flat_v,
            places[part.start], sizes[part], carried,
        )

    for chunk in range(count):
        got = send(own[chunk], TO_MIDS)
        if chunk >= 2:
            got = tie(got, totals[chunk - 2])
        total = own[chunk] + got
        total = total + send(total, ACROSS)
        if chunk in early:
            total = tie(total, early[chunk])
        if chunk == count - 2:
            carried = move(groups[0], carried)
            total = tie(total, carried[1])
        totals.append(total)
        backs.append(send(total, TO_ENDS))
    for part in groups[1:]:
        carried = move(part, carried)
    spread_v = next_spread_v
    flat_v = carried[0]
    line_sq = placed(jnp.sum(carried[1], axis=(1, 2)), hit)
    spread_sq = lax.optimization_barrier(placed(jnp.sum(spread_sq, axis=(1, 2)), spread_hit))
    factor, line_factor = factors(spread_sq + line_sq)

    order = [jnp.where(is_low, LINE - 1 - place, place) for place in range(LINE)]
    block = step_blocks(order[:1], line_factor, flat, flat_v, rest)
    block += step_blocks(order[1:], line_factor, flat, tie(flat_v, block[0]), rest)
    arrived = [send(block[place], TO_MIDS) for place in range(3)]
    passed = [send(block[place] + arrived[place], ACROSS) for place in range(2)]
    last = send(block[3] + passed[0], TO_ENDS)
    buffer = end_spread(share, factor, spread, spread_v, rows)
    place = o.astype(jnp.int32).reshape(1)
    end_parts, mid_parts = [block[3], last], [block[2], arrived[2], passed[1]]
    return end_line(share, place, end_flag, flat_v, end_parts, mid_parts, buffer, cut)


def solution(mesh):
    in_specs = (P("worker", "outer", None, "mp"), P(("worker", "outer"), "mp"), P())
    out_specs = P(("worker", "outer"), "mp")

    return jax.shard_map(on_device, mesh=mesh, in_specs=in_specs, out_specs=out_specs, check_vma=False)
```

```python
import math

import jax
import jax.numpy as jnp
from jax import lax
from jax.experimental import pallas as pl
from jax.experimental.pallas import tpu as pltpu
from jax.sharding import PartitionSpec as P


D = 3584
ITERS = 2
KVW = 4096
AXES = ("worker", "outer", "mp")
LINE = 4
TILE = 8
SPREAD = 0.4

GRANT = 60 << 20

epsilon = 1e-06


def sum_over_devices(value):
    for axis in AXES:
        size = lax.axis_size(axis)
        step = 1
        while step < size:
            value = value + lax.ppermute(value, axis, [(i, i ^ step) for i in range(size)])
            step *= 2
    return value


def send(value, pairs, axis="outer"):
    return lax.ppermute(value, axis, pairs)


TO_MIDS = [(0, 1), (3, 2)]
ACROSS = [(1, 2), (2, 1)]
TO_ENDS = [(1, 0), (2, 3)]


def tie(value, earlier):
    return lax.optimization_barrier((value, earlier))[0]


def split(rows, outers):
    cut = int(rows * SPREAD) // TILE * TILE
    rest = rows - cut
    tiles = rest // TILE
    if outers != LINE or rest % TILE or tiles < 13 or not cut:
        return None
    body = tiles - 10
    sizes = [1, 2] + [3] * (body // 3) + [body % 3] * (body % 3 > 0) + [2, 2, 1, 1, 1]
    return cut, sizes


SMEM = pl.BlockSpec(memory_space=pltpu.SMEM)


def run(kernel, grid, in_specs, out_specs, out_shape, operands, moved, aliases={}, prefetch=0):
    return pl.pallas_call(
        kernel,
        grid_spec=pltpu.PrefetchScalarGridSpec(
            num_scalar_prefetch=prefetch, grid=grid, in_specs=in_specs, out_specs=out_specs
        ),
        out_shape=out_shape,
        input_output_aliases=aliases,
        compiler_params=pltpu.CompilerParams(vmem_limit_bytes=GRANT),
        cost_estimate=pl.CostEstimate(flops=4 * moved, bytes_accessed=4 * moved, transcendentals=0),
    )(*operands)


def group_spec(begin, count, tile, columns):
    return pl.BlockSpec((tile, columns), lambda i: (jnp.clip(i - begin, 0, count - 1), 0))


def begins(sizes):
    return [sum(sizes[:i]) for i in range(len(sizes))]


def step_of(factor, values, v):
    return sum(factor[i] * (value[...] - v) for i, value in enumerate(values))


def step_chunks(factor, values, v, start, sizes):
    columns, tile, count = v.shape[1], TILE * LINE, len(values)
    places = begins(sizes)

    def kernel(factor, *refs):
        values, v, outs = refs[:count], refs[count], refs[count + 1 :]
        i = pl.program_id(0)
        total = step_of(factor, values, v[...])
        for out, begin, size in zip(outs, places, sizes):

            @pl.when((i >= begin) & (i < begin + size))
            def _(out=out):
                out[...] = total

    at = pl.BlockSpec((tile, columns), lambda i: (start + i, 0))
    outs = [group_spec(begin, size, tile, columns) for begin, size in zip(places, sizes)]
    shapes = [jax.ShapeDtypeStruct((size * tile, columns), v.dtype) for size in sizes]
    moved = (count + 2) * sum(sizes) * tile * columns
    in_specs = [SMEM] + [at] * (count + 1)
    return run(kernel, (sum(sizes),), in_specs, outs, shapes, (factor, *values, v), moved)


def move_chunks(is_end, share, totals, backs, values, v, start, sizes, carried):
    columns, tile, count, chunks = v.shape[1], TILE * LINE, len(values), len(sizes)
    places = begins(sizes)

    def kernel(is_end, v, *refs):
        values, rest = refs[:count], refs[count:]
        totals, backs, (v_out, sq_out) = rest[:chunks], rest[chunks : 2 * chunks], rest[-2:]
        i = pl.program_id(0)

        @pl.when(i == 0)
        def _():
            sq_out[...] = rest[-3][...] if carried else jnp.zeros_like(sq_out)

        for total, back, begin, size in zip(totals, backs, places, sizes):

            @pl.when((i >= begin) & (i < begin + size))
            def _(total=total, back=back):
                step = jnp.where(is_end[0] > 0, back[...], total[...])
                v_out[...] = v[...] + step * share

        moved = v_out[...]
        for k, value in enumerate(values):
            square = jnp.square(value[...] - moved)
            folded = sum(square[j : j + 8] for j in range(0, tile, 8))
            sq_out[k] += sum(folded[:, j : j + 128] for j in range(0, columns, 128))

    at = pl.BlockSpec((tile, columns), lambda i: (start + i, 0))
    squares = pl.BlockSpec((count, 8, 128), lambda i: (0, 0, 0))
    parts = [group_spec(begin, size, tile, columns) for begin, size in zip(places, sizes)]
    in_specs = [SMEM] + [at] * (count + 1) + parts + parts
    operands = (is_end, v, *values, *totals, *backs)
    aliases = {}
    if carried:
        in_specs += [pl.BlockSpec(memory_space=pl.ANY), squares]
        aliases = {len(operands): 0, len(operands) + 1: 1}
        operands += tuple(carried)
    shapes = (
        jax.ShapeDtypeStruct(v.shape, v.dtype),
        jax.ShapeDtypeStruct((count, 8, 128), v.dtype),
    )
    moved = (count + 4) * sum(sizes) * tile * columns
    return run(kernel, (sum(sizes),), in_specs, (at, squares), shapes, operands, moved, aliases)


def step_blocks(places, factor, values, v):
    _, rest, columns = v.shape
    count, blocks, parts = len(values), len(places), 4
    width = columns // parts

    def kernel(places, factor, *refs):
        values, v, outs = refs[:count], refs[count], refs[count + 1 :]
        total = step_of(factor, values, v[...])
        for k, out in enumerate(outs):

            @pl.when(pl.program_id(0) == k)
            def _(out=out):
                out[...] = total

    at = pl.BlockSpec((None, rest, width), lambda b, i, places: (places[b], 0, i))
    outs = [
        pl.BlockSpec(
            (rest, width), lambda b, i, _, k=k: (0, jnp.clip((b - k) * parts + i, 0, parts - 1))
        )
        for k in range(blocks)
    ]
    shapes = [jax.ShapeDtypeStruct((rest, columns), v.dtype)] * blocks
    moved = (count + 2) * blocks * rest * columns
    operands = (jnp.stack(places).astype(jnp.int32), factor, *values, v)
    in_specs = [SMEM] + [at] * (count + 1)
    return run(kernel, (blocks, parts), in_specs, outs, shapes, operands, moved, prefetch=1)


def move_spread(share, factor, values, v):
    (rows, columns), count = v.shape, values.shape[0]

    def kernel(factor, v, values, v_out, sq_out):
        base = v[...]
        moved = base + sum(factor[k] * (values[k] - base) for k in range(count)) * share
        v_out[...] = moved

        @pl.when(pl.program_id(0) == 0)
        def _():
            sq_out[...] = jnp.zeros_like(sq_out)

        for k in range(count):
            square = jnp.square(values[k] - moved)
            sq_out[k] += sum(square[:, j : j + 128] for j in range(0, columns, 128))

    at = pl.BlockSpec((TILE, columns), lambda i: (i, 0))
    stack = pl.BlockSpec((count, TILE, columns), lambda i: (0, i, 0))
    squares = pl.BlockSpec((count, TILE, 128), lambda i: (0, 0, 0))
    shapes = (
        jax.ShapeDtypeStruct(v.shape, v.dtype),
        jax.ShapeDtypeStruct((count, TILE, 128), v.dtype),
    )
    moved = (count + 2) * rows * columns
    operands = (factor, v, values)
    return run(kernel, (rows // TILE,), [SMEM, at, stack], (at, squares), shapes, operands, moved)


def spread_only(mine, center, radius_total, worker_count):
    own_rows = center
    gathered = lax.all_to_all(mine, ("worker", "outer"), split_axis=0, concat_axis=0, tiled=True)
    for _ in range(ITERS):
        difference = gathered - own_rows[None]
        norm_sq = sum_over_devices(jnp.sum(difference * difference, axis=(1, 2)))
        factor = jnp.minimum(1.0, radius_total * lax.rsqrt(norm_sq + epsilon))
        own_rows = own_rows + jnp.sum(factor[:, None, None] * difference, axis=0) / worker_count
    return own_rows


def on_device(grads, center, radius):
    workers, outers = lax.axis_size("worker"), lax.axis_size("outer")
    worker_count = workers * outers
    radius_total = radius[0] * math.sqrt(D * KVW)
    rows, columns = center.shape
    mine = grads.reshape(worker_count, rows, columns)
    plan = split(rows, outers)
    if plan is None:
        return spread_only(mine, center, radius_total, worker_count)
    cut, sizes = plan
    rest = rows - cut

    w, o = lax.axis_index("worker"), lax.axis_index("outer")
    is_end = (o == 0) | (o == LINE - 1)
    is_low = o < LINE // 2

    def line_rows(source, worker):
        return lax.dynamic_slice(source, (worker * outers, cut, 0), (outers, rest, columns))

    tail = center[cut:]
    pair = send(tail, [(i, i ^ 1) for i in range(LINE)])
    steps = list(range(workers // 2, workers)) + list(range(1, workers // 2)) + [0]
    held, source = [], mine
    for step in steps:
        sent = line_rows(source, w ^ step)
        source = tie(source, sent)
        if step:
            swap = [(i, i ^ step) for i in range(workers)]
            sent = send(sent, swap, "worker")
        held.append(sent)
    spread = lax.all_to_all(
        mine[:, :cut], ("worker", "outer"), split_axis=0, concat_axis=0, tiled=True
    )
    first = (o % 2) == 0
    near = jnp.where(first, jnp.stack([tail, pair]), jnp.stack([pair, tail]))
    crossed = send(near, ACROSS)
    far = jnp.where(is_end, send(crossed, TO_ENDS), crossed)
    line_v = jnp.where(is_low, jnp.concatenate([near, far]), jnp.concatenate([far, near]))
    spread_v, share = center[:cut], 1 / worker_count

    places = jnp.stack([(w ^ step) * outers + o for step in steps])
    hit = places[:, None] == jnp.arange(worker_count)[None]

    def placed(line_sq):
        return jnp.sum(jnp.where(hit, line_sq[:, None], 0.0), axis=0)

    def factors(both):
        norm_sq = sum_over_devices(both)
        factor = jnp.minimum(1.0, radius_total * lax.rsqrt(norm_sq + epsilon))
        return factor, jnp.sum(jnp.where(hit, factor[None], 0.0), axis=1)

    line_sq, v = jnp.zeros((worker_count,), jnp.float32), line_v
    for place in reversed(range(workers)):
        square = jnp.sum(jnp.square(held[place] - v))
        line_sq = lax.optimization_barrier(line_sq + jnp.where(hit[place], square, 0.0))
        v = tie(v, line_sq)
    spread_sq = jnp.sum(jnp.square(spread - spread_v[None]), axis=(1, 2))
    factor, line_factor = factors(spread_sq + line_sq)

    flat = [value.reshape(outers * rest, columns) for value in held]
    flat_v = line_v.reshape(outers * rest, columns)
    end_flag = is_end.astype(jnp.int32).reshape(1)
    next_spread_v, spread_sq = move_spread(share, factor, spread, spread_v)
    early = {2: next_spread_v}
    count, places = len(sizes), begins(sizes)
    own = step_chunks(line_factor, flat, flat_v, 0, sizes[:1])
    own += step_chunks(line_factor, flat, tie(flat_v, own[0]), places[1], sizes[1:2])
    own += step_chunks(line_factor, flat, tie(flat_v, own[1]), places[2], sizes[2:])
    cuts = [0, count - 6, count - 4, count - 2, count]
    groups = [slice(*pair) for pair in zip(cuts, cuts[1:])]
    totals, backs, carried = [], [], ()

    def move(part, carried):
        return move_chunks(
            end_flag, share, totals[part], backs[part], flat, flat_v,
            places[part.start], sizes[part], carried,
        )

    for chunk in range(count):
        got = send(own[chunk], TO_MIDS)
        if chunk >= 2:
            got = tie(got, totals[chunk - 2])
        total = own[chunk] + got
        total = total + send(total, ACROSS)
        if chunk in early:
            total = tie(total, early[chunk])
        if chunk in (count - 4, count - 1):
            carried = move(groups[chunk == count - 1], carried)
            total = tie(total, carried[1])
        totals.append(total)
        backs.append(send(total, TO_ENDS))
    for part in groups[2:]:
        carried = move(part, carried)
    spread_v = next_spread_v
    flat_v = carried[0]
    line_v = flat_v.reshape(line_v.shape)
    spread_sq = lax.optimization_barrier(jnp.sum(spread_sq, axis=(1, 2)))
    factor, line_factor = factors(spread_sq + placed(jnp.sum(carried[1], axis=(1, 2))))

    order = [jnp.where(is_low, LINE - 1 - place, place) for place in range(LINE)]
    block = step_blocks(order[:1], line_factor, held, line_v)
    block += step_blocks(order[1:], line_factor, held, tie(line_v, block[0]))
    arrived = [send(block[place], TO_MIDS) for place in range(3)]
    passed = [send(block[place] + arrived[place], ACROSS) for place in range(2)]
    end_sum = block[3] + send(block[3] + passed[0], TO_ENDS)
    mid_sum = block[2] + arrived[2] + passed[1]
    own_v = lax.dynamic_index_in_dim(line_v, o, 0, keepdims=False)
    own_v = own_v + jnp.where(is_end, end_sum, mid_sum) * share
    step = jnp.sum(factor[:, None, None] * (spread - spread_v[None]), axis=0)
    return jnp.concatenate([spread_v + step * share, own_v])


def solution(mesh):
    in_specs = (P("worker", "outer", None, "mp"), P(("worker", "outer"), "mp"), P())
    out_specs = P(("worker", "outer"), "mp")

    return jax.shard_map(on_device, mesh=mesh, in_specs=in_specs, out_specs=out_specs, check_vma=False)
```

```python
import math

import jax
import jax.numpy as jnp
from jax import lax
from jax.experimental import pallas as pl
from jax.experimental.pallas import tpu as pltpu
from jax.sharding import PartitionSpec as P


D = 3584
ITERS = 2
KVW = 4096
AXES = ("worker", "outer", "mp")
LINE = 4
TILE = 8
SPREAD = 3 / 7

GRANT = 60 << 20

epsilon = 1e-06


def sum_over_devices(value):
    for axis in AXES:
        size = lax.axis_size(axis)
        step = 1
        while step < size:
            value = value + lax.ppermute(value, axis, [(i, i ^ step) for i in range(size)])
            step *= 2
    return value


def send(value, pairs, axis="outer"):
    return lax.ppermute(value, axis, pairs)


TO_MIDS = [(0, 1), (3, 2)]
ACROSS = [(1, 2), (2, 1)]
TO_ENDS = [(1, 0), (2, 3)]


def tie(value, earlier):
    return lax.optimization_barrier((value, earlier))[0]


def split(rows, outers):
    cut = int(rows * SPREAD) // TILE * TILE
    rest = rows - cut
    tiles = rest // TILE
    if outers != LINE or rest % TILE or tiles < 13 or not cut:
        return None
    body = tiles - 10
    sizes = [1, 2, 2] + [3] * (body // 3) + [body % 3] * (body % 3 > 0) + [2, 2, 1]
    return cut, sizes


SMEM = pl.BlockSpec(memory_space=pltpu.SMEM)


def run(kernel, grid, in_specs, out_specs, out_shape, operands, moved, aliases={}, prefetch=0):
    return pl.pallas_call(
        kernel,
        grid_spec=pltpu.PrefetchScalarGridSpec(
            num_scalar_prefetch=prefetch, grid=grid, in_specs=in_specs, out_specs=out_specs
        ),
        out_shape=out_shape,
        input_output_aliases=aliases,
        compiler_params=pltpu.CompilerParams(vmem_limit_bytes=GRANT),
        cost_estimate=pl.CostEstimate(flops=4 * moved, bytes_accessed=4 * moved, transcendentals=0),
    )(*operands)


def group_spec(begin, count, tile, columns):
    return pl.BlockSpec((tile, columns), lambda i: (jnp.clip(i - begin, 0, count - 1), 0))


def begins(sizes):
    return [sum(sizes[:i]) for i in range(len(sizes))]


def step_of(factor, values, v):
    return sum(factor[i] * (value[...] - v) for i, value in enumerate(values))


def step_chunks(factor, values, v, start, sizes):
    columns, tile, count = v.shape[1], TILE * LINE, len(values)
    places = begins(sizes)

    def kernel(factor, *refs):
        values, v, outs = refs[:count], refs[count], refs[count + 1 :]
        i = pl.program_id(0)
        total = step_of(factor, values, v[...])
        for out, begin, size in zip(outs, places, sizes):

            @pl.when((i >= begin) & (i < begin + size))
            def _(out=out):
                out[...] = total

    at = pl.BlockSpec((tile, columns), lambda i: (start + i, 0))
    outs = [group_spec(begin, size, tile, columns) for begin, size in zip(places, sizes)]
    shapes = [jax.ShapeDtypeStruct((size * tile, columns), v.dtype) for size in sizes]
    moved = (count + 2) * sum(sizes) * tile * columns
    in_specs = [SMEM] + [at] * (count + 1)
    return run(kernel, (sum(sizes),), in_specs, outs, shapes, (factor, *values, v), moved)


def move_chunks(is_end, share, totals, backs, values, v, start, sizes, carried):
    columns, tile, count, chunks = v.shape[1], TILE * LINE, len(values), len(sizes)
    places = begins(sizes)

    def kernel(is_end, v, *refs):
        values, rest = refs[:count], refs[count:]
        totals, backs, (v_out, sq_out) = rest[:chunks], rest[chunks : 2 * chunks], rest[-2:]
        i = pl.program_id(0)

        @pl.when(i == 0)
        def _():
            sq_out[...] = rest[-3][...] if carried else jnp.zeros_like(sq_out)

        for total, back, begin, size in zip(totals, backs, places, sizes):

            @pl.when((i >= begin) & (i < begin + size))
            def _(total=total, back=back):
                step = jnp.where(is_end[0] > 0, back[...], total[...])
                v_out[...] = v[...] + step * share

        moved = v_out[...]
        for k, value in enumerate(values):
            square = jnp.square(value[...] - moved)
            folded = sum(square[j : j + 8] for j in range(0, tile, 8))
            sq_out[k] += sum(folded[:, j : j + 128] for j in range(0, columns, 128))

    at = pl.BlockSpec((tile, columns), lambda i: (start + i, 0))
    squares = pl.BlockSpec((count, 8, 128), lambda i: (0, 0, 0))
    parts = [group_spec(begin, size, tile, columns) for begin, size in zip(places, sizes)]
    in_specs = [SMEM] + [at] * (count + 1) + parts + parts
    operands = (is_end, v, *values, *totals, *backs)
    aliases = {}
    if carried:
        in_specs += [pl.BlockSpec(memory_space=pl.ANY), squares]
        aliases = {len(operands): 0, len(operands) + 1: 1}
        operands += tuple(carried)
    shapes = (
        jax.ShapeDtypeStruct(v.shape, v.dtype),
        jax.ShapeDtypeStruct((count, 8, 128), v.dtype),
    )
    moved = (count + 4) * sum(sizes) * tile * columns
    return run(kernel, (sum(sizes),), in_specs, (at, squares), shapes, operands, moved, aliases)


def step_blocks(places, factor, values, v):
    _, rest, columns = v.shape
    count, blocks, parts = len(values), len(places), 4
    width = columns // parts

    def kernel(places, factor, *refs):
        values, v, outs = refs[:count], refs[count], refs[count + 1 :]
        total = step_of(factor, values, v[...])
        for k, out in enumerate(outs):

            @pl.when(pl.program_id(0) == k)
            def _(out=out):
                out[...] = total

    at = pl.BlockSpec((None, rest, width), lambda b, i, places: (places[b], 0, i))
    outs = [
        pl.BlockSpec(
            (rest, width), lambda b, i, _, k=k: (0, jnp.clip((b - k) * parts + i, 0, parts - 1))
        )
        for k in range(blocks)
    ]
    shapes = [jax.ShapeDtypeStruct((rest, columns), v.dtype)] * blocks
    moved = (count + 2) * blocks * rest * columns
    operands = (jnp.stack(places).astype(jnp.int32), factor, *values, v)
    in_specs = [SMEM] + [at] * (count + 1)
    return run(kernel, (blocks, parts), in_specs, outs, shapes, operands, moved, prefetch=1)


def move_spread(share, factor, values, v):
    (rows, columns), count = v.shape, values.shape[0]
    tile = 2 * TILE if rows % (2 * TILE) == 0 else TILE

    def kernel(factor, v, values, v_out, sq_out):
        base = v[...]
        moved = base + sum(factor[k] * (values[k] - base) for k in range(count)) * share
        v_out[...] = moved

        @pl.when(pl.program_id(0) == 0)
        def _():
            sq_out[...] = jnp.zeros_like(sq_out)

        for k in range(count):
            square = jnp.square(values[k] - moved)
            folded = sum(square[j : j + TILE] for j in range(0, tile, TILE))
            sq_out[k] += sum(folded[:, j : j + 128] for j in range(0, columns, 128))

    at = pl.BlockSpec((tile, columns), lambda i: (i, 0))
    stack = pl.BlockSpec((count, tile, columns), lambda i: (0, i, 0))
    squares = pl.BlockSpec((count, TILE, 128), lambda i: (0, 0, 0))
    shapes = (
        jax.ShapeDtypeStruct(v.shape, v.dtype),
        jax.ShapeDtypeStruct((count, TILE, 128), v.dtype),
    )
    moved = (count + 2) * rows * columns
    operands = (factor, v, values)
    return run(kernel, (rows // tile,), [SMEM, at, stack], (at, squares), shapes, operands, moved)


def spread_only(mine, center, radius_total, worker_count):
    own_rows = center
    gathered = lax.all_to_all(mine, ("worker", "outer"), split_axis=0, concat_axis=0, tiled=True)
    for _ in range(ITERS):
        difference = gathered - own_rows[None]
        norm_sq = sum_over_devices(jnp.sum(difference * difference, axis=(1, 2)))
        factor = jnp.minimum(1.0, radius_total * lax.rsqrt(norm_sq + epsilon))
        own_rows = own_rows + jnp.sum(factor[:, None, None] * difference, axis=0) / worker_count
    return own_rows


def on_device(grads, center, radius):
    workers, outers = lax.axis_size("worker"), lax.axis_size("outer")
    worker_count = workers * outers
    radius_total = radius[0] * math.sqrt(D * KVW)
    rows, columns = center.shape
    mine = grads.reshape(worker_count, rows, columns)
    plan = split(rows, outers)
    if plan is None:
        return spread_only(mine, center, radius_total, worker_count)
    cut, sizes = plan
    rest = rows - cut

    w, o = lax.axis_index("worker"), lax.axis_index("outer")
    is_end = (o == 0) | (o == LINE - 1)
    is_low = o < LINE // 2

    def line_rows(source, worker):
        return lax.dynamic_slice(source, (worker * outers, cut, 0), (outers, rest, columns))

    tail = center[cut:]
    pair = send(tail, [(i, i ^ 1) for i in range(LINE)])
    steps = list(range(workers // 2, workers)) + list(range(1, workers // 2)) + [0]
    held, source = [], mine
    for step in steps:
        sent = line_rows(source, w ^ step)
        source = tie(source, sent)
        if step:
            swap = [(i, i ^ step) for i in range(workers)]
            sent = send(sent, swap, "worker")
        held.append(sent)
    spread = lax.all_to_all(
        mine[:, :cut], ("worker", "outer"), split_axis=0, concat_axis=0, tiled=True
    )
    first = (o % 2) == 0
    near = [jnp.where(first, tail, pair), jnp.where(first, pair, tail)]
    far = []
    for part in (tail, pair):
        crossed = send(part, ACROSS)
        far.append(jnp.where(is_end, send(crossed, TO_ENDS), crossed))
    low, high = near + far, far[::-1] + near
    line_v = jnp.stack([jnp.where(is_low, *parts) for parts in zip(low, high)])
    spread_v, share = center[:cut], 1 / worker_count

    places = jnp.stack([(w ^ step) * outers + o for step in steps])
    hit = places[:, None] == jnp.arange(worker_count)[None]

    def placed(line_sq):
        return jnp.sum(jnp.where(hit, line_sq[:, None], 0.0), axis=0)

    def factors(both):
        norm_sq = sum_over_devices(both)
        factor = jnp.minimum(1.0, radius_total * lax.rsqrt(norm_sq + epsilon))
        return factor, jnp.sum(jnp.where(hit, factor[None], 0.0), axis=1)

    line_sq, v = jnp.zeros((worker_count,), jnp.float32), line_v
    for place in reversed(range(workers)):
        square = jnp.sum(jnp.square(held[place] - v))
        line_sq = lax.optimization_barrier(line_sq + jnp.where(hit[place], square, 0.0))
        v = tie(v, line_sq)
    spread_sq = jnp.sum(jnp.square(spread - spread_v[None]), axis=(1, 2))
    factor, line_factor = factors(spread_sq + line_sq)

    flat = [value.reshape(outers * rest, columns) for value in held]
    flat_v = line_v.reshape(outers * rest, columns)
    end_flag = is_end.astype(jnp.int32).reshape(1)
    next_spread_v, spread_sq = move_spread(share, factor, spread, spread_v)
    early = {2: next_spread_v}
    count, places = len(sizes), begins(sizes)
    own = step_chunks(line_factor, flat, flat_v, 0, sizes[:1])
    own += step_chunks(line_factor, flat, tie(flat_v, own[0]), places[1], sizes[1:2])
    own += step_chunks(line_factor, flat, tie(flat_v, own[1]), places[2], sizes[2:4])
    own += step_chunks(line_factor, flat, tie(flat_v, own[2]), places[4], sizes[4:])
    cuts = [0, count - 5, count - 3, count - 1, count]
    groups = [slice(*pair) for pair in zip(cuts, cuts[1:])]
    totals, backs, carried = [], [], ()

    def move(part, carried):
        return move_chunks(
            end_flag, share, totals[part], backs[part], flat, flat_v,
            places[part.start], sizes[part], carried,
        )

    for chunk in range(count):
        got = send(own[chunk], TO_MIDS)
        if chunk >= 2:
            got = tie(got, totals[chunk - 2])
        total = own[chunk] + got
        total = total + send(total, ACROSS)
        if chunk in early:
            total = tie(total, early[chunk])
        if chunk in (count - 3, count - 1):
            carried = move(groups[chunk == count - 1], carried)
            total = tie(total, carried[1])
        totals.append(total)
        backs.append(send(total, TO_ENDS))
    for part in groups[2:]:
        carried = move(part, carried)
    spread_v = next_spread_v
    flat_v = carried[0]
    line_v = flat_v.reshape(line_v.shape)
    spread_sq = lax.optimization_barrier(jnp.sum(spread_sq, axis=(1, 2)))
    factor, line_factor = factors(spread_sq + placed(jnp.sum(carried[1], axis=(1, 2))))

    order = [jnp.where(is_low, LINE - 1 - place, place) for place in range(LINE)]
    block = step_blocks(order[:1], line_factor, held, line_v)
    block += step_blocks(order[1:], line_factor, held, tie(line_v, block[0]))
    arrived = [send(block[place], TO_MIDS) for place in range(3)]
    passed = [send(block[place] + arrived[place], ACROSS) for place in range(2)]
    end_sum = block[3] + send(block[3] + passed[0], TO_ENDS)
    mid_sum = block[2] + arrived[2] + passed[1]
    own_v = lax.dynamic_index_in_dim(line_v, o, 0, keepdims=False)
    own_v = own_v + jnp.where(is_end, end_sum, mid_sum) * share
    step = jnp.sum(factor[:, None, None] * (spread - spread_v[None]), axis=0)
    return jnp.concatenate([spread_v + step * share, own_v])


def solution(mesh):
    in_specs = (P("worker", "outer", None, "mp"), P(("worker", "outer"), "mp"), P())
    out_specs = P(("worker", "outer"), "mp")

    return jax.shard_map(on_device, mesh=mesh, in_specs=in_specs, out_specs=out_specs, check_vma=False)
```

```python
import math

import jax
import jax.numpy as jnp
from jax import lax
from jax.experimental import pallas as pl
from jax.experimental.pallas import tpu as pltpu
from jax.sharding import PartitionSpec as P


D = 3584
ITERS = 2
KVW = 4096
AXES = ("worker", "outer", "mp")
LINE = 4
TILE = 8
SPREAD = 3 / 7

GRANT = 60 << 20

epsilon = 1e-06


def sum_over_devices(value):
    for axis in AXES:
        size = lax.axis_size(axis)
        step = 1
        while step < size:
            value = value + lax.ppermute(value, axis, [(i, i ^ step) for i in range(size)])
            step *= 2
    return value


def send(value, pairs, axis="outer"):
    return lax.ppermute(value, axis, pairs)


TO_MIDS = [(0, 1), (3, 2)]
ACROSS = [(1, 2), (2, 1)]
TO_ENDS = [(1, 0), (2, 3)]


def tie(value, earlier):
    return lax.optimization_barrier((value, earlier))[0]


def split(rows, outers):
    cut = int(rows * SPREAD) // TILE * TILE
    rest = rows - cut
    tiles = rest // TILE
    if outers != LINE or rest % TILE or tiles < 13 or not cut:
        return None
    sizes = [1] + [2] * ((tiles - 2) // 2) + [1] * (tiles % 2) + [1]
    return cut, sizes


SMEM = pl.BlockSpec(memory_space=pltpu.SMEM)


def run(kernel, grid, in_specs, out_specs, out_shape, operands, moved, aliases={}, prefetch=0):
    return pl.pallas_call(
        kernel,
        grid_spec=pltpu.PrefetchScalarGridSpec(
            num_scalar_prefetch=prefetch, grid=grid, in_specs=in_specs, out_specs=out_specs
        ),
        out_shape=out_shape,
        input_output_aliases=aliases,
        compiler_params=pltpu.CompilerParams(vmem_limit_bytes=GRANT),
        cost_estimate=pl.CostEstimate(flops=4 * moved, bytes_accessed=4 * moved, transcendentals=0),
    )(*operands)


def group_spec(begin, count, tile, columns):
    return pl.BlockSpec((tile, columns), lambda i: (jnp.clip(i - begin, 0, count - 1), 0))


def begins(sizes):
    return [sum(sizes[:i]) for i in range(len(sizes))]


def step_of(factor, values, v):
    return sum(factor[i] * (value[...] - v) for i, value in enumerate(values))


def step_chunks(factor, values, v, start, sizes):
    columns, tile, count = v.shape[1], TILE * LINE, len(values)
    places = begins(sizes)

    def kernel(factor, *refs):
        values, v, outs = refs[:count], refs[count], refs[count + 1 :]
        i = pl.program_id(0)
        total = step_of(factor, values, v[...])
        for out, begin, size in zip(outs, places, sizes):

            @pl.when((i >= begin) & (i < begin + size))
            def _(out=out):
                out[...] = total

    at = pl.BlockSpec((tile, columns), lambda i: (start + i, 0))
    outs = [group_spec(begin, size, tile, columns) for begin, size in zip(places, sizes)]
    shapes = [jax.ShapeDtypeStruct((size * tile, columns), v.dtype) for size in sizes]
    moved = (count + 2) * sum(sizes) * tile * columns
    in_specs = [SMEM] + [at] * (count + 1)
    return run(kernel, (sum(sizes),), in_specs, outs, shapes, (factor, *values, v), moved)


def move_chunks(is_end, share, totals, backs, values, v, start, sizes, carried):
    columns, tile, count, chunks = v.shape[1], TILE * LINE, len(values), len(sizes)
    places = begins(sizes)

    def kernel(is_end, v, *refs):
        values, rest = refs[:count], refs[count:]
        totals, backs, (v_out, sq_out) = rest[:chunks], rest[chunks : 2 * chunks], rest[-2:]
        i = pl.program_id(0)

        @pl.when(i == 0)
        def _():
            sq_out[...] = rest[-3][...] if carried else jnp.zeros_like(sq_out)

        for total, back, begin, size in zip(totals, backs, places, sizes):

            @pl.when((i >= begin) & (i < begin + size))
            def _(total=total, back=back):
                step = jnp.where(is_end[0] > 0, back[...], total[...])
                v_out[...] = v[...] + step * share

        moved = v_out[...]
        for k, value in enumerate(values):
            square = jnp.square(value[...] - moved)
            folded = sum(square[j : j + 8] for j in range(0, tile, 8))
            sq_out[k] += sum(folded[:, j : j + 128] for j in range(0, columns, 128))

    at = pl.BlockSpec((tile, columns), lambda i: (start + i, 0))
    squares = pl.BlockSpec((count, 8, 128), lambda i: (0, 0, 0))
    parts = [group_spec(begin, size, tile, columns) for begin, size in zip(places, sizes)]
    in_specs = [SMEM] + [at] * (count + 1) + parts + parts
    operands = (is_end, v, *values, *totals, *backs)
    aliases = {}
    if carried:
        in_specs += [pl.BlockSpec(memory_space=pl.ANY), squares]
        aliases = {len(operands): 0, len(operands) + 1: 1}
        operands += tuple(carried)
    shapes = (
        jax.ShapeDtypeStruct(v.shape, v.dtype),
        jax.ShapeDtypeStruct((count, 8, 128), v.dtype),
    )
    moved = (count + 4) * sum(sizes) * tile * columns
    return run(kernel, (sum(sizes),), in_specs, (at, squares), shapes, operands, moved, aliases)


def step_blocks(places, factor, values, v):
    _, rest, columns = v.shape
    count, blocks, parts = len(values), len(places), 4
    width = columns // parts

    def kernel(places, factor, *refs):
        values, v, outs = refs[:count], refs[count], refs[count + 1 :]
        total = step_of(factor, values, v[...])
        for k, out in enumerate(outs):

            @pl.when(pl.program_id(0) == k)
            def _(out=out):
                out[...] = total

    at = pl.BlockSpec((None, rest, width), lambda b, i, places: (places[b], 0, i))
    outs = [
        pl.BlockSpec(
            (rest, width), lambda b, i, _, k=k: (0, jnp.clip((b - k) * parts + i, 0, parts - 1))
        )
        for k in range(blocks)
    ]
    shapes = [jax.ShapeDtypeStruct((rest, columns), v.dtype)] * blocks
    moved = (count + 2) * blocks * rest * columns
    operands = (jnp.stack(places).astype(jnp.int32), factor, *values, v)
    in_specs = [SMEM] + [at] * (count + 1)
    return run(kernel, (blocks, parts), in_specs, outs, shapes, operands, moved, prefetch=1)


def move_spread(share, factor, values, v):
    (rows, columns), count = v.shape, values.shape[0]
    tile = 2 * TILE if rows % (2 * TILE) == 0 else TILE

    def kernel(factor, v, values, v_out, sq_out):
        base = v[...]
        moved = base + sum(factor[k] * (values[k] - base) for k in range(count)) * share
        v_out[...] = moved

        @pl.when(pl.program_id(0) == 0)
        def _():
            sq_out[...] = jnp.zeros_like(sq_out)

        for k in range(count):
            square = jnp.square(values[k] - moved)
            folded = sum(square[j : j + TILE] for j in range(0, tile, TILE))
            sq_out[k] += sum(folded[:, j : j + 128] for j in range(0, columns, 128))

    at = pl.BlockSpec((tile, columns), lambda i: (i, 0))
    stack = pl.BlockSpec((count, tile, columns), lambda i: (0, i, 0))
    squares = pl.BlockSpec((count, TILE, 128), lambda i: (0, 0, 0))
    shapes = (
        jax.ShapeDtypeStruct(v.shape, v.dtype),
        jax.ShapeDtypeStruct((count, TILE, 128), v.dtype),
    )
    moved = (count + 2) * rows * columns
    operands = (factor, v, values)
    return run(kernel, (rows // tile,), [SMEM, at, stack], (at, squares), shapes, operands, moved)


def spread_only(mine, center, radius_total, worker_count):
    own_rows = center
    gathered = lax.all_to_all(mine, ("worker", "outer"), split_axis=0, concat_axis=0, tiled=True)
    for _ in range(ITERS):
        difference = gathered - own_rows[None]
        norm_sq = sum_over_devices(jnp.sum(difference * difference, axis=(1, 2)))
        factor = jnp.minimum(1.0, radius_total * lax.rsqrt(norm_sq + epsilon))
        own_rows = own_rows + jnp.sum(factor[:, None, None] * difference, axis=0) / worker_count
    return own_rows


def on_device(grads, center, radius):
    workers, outers = lax.axis_size("worker"), lax.axis_size("outer")
    worker_count = workers * outers
    radius_total = radius[0] * math.sqrt(D * KVW)
    rows, columns = center.shape
    mine = grads.reshape(worker_count, rows, columns)
    plan = split(rows, outers)
    if plan is None:
        return spread_only(mine, center, radius_total, worker_count)
    cut, sizes = plan
    rest = rows - cut

    w, o = lax.axis_index("worker"), lax.axis_index("outer")
    is_end = (o == 0) | (o == LINE - 1)
    is_low = o < LINE // 2

    def line_rows(source, worker):
        return lax.dynamic_slice(source, (worker * outers, cut, 0), (outers, rest, columns))

    tail = center[cut:]
    pair = send(tail, [(i, i ^ 1) for i in range(LINE)])
    steps = list(range(workers // 2, workers)) + list(range(1, workers // 2)) + [0]
    held, source = [], mine
    for step in steps:
        sent = line_rows(source, w ^ step)
        source = tie(source, sent)
        if step:
            swap = [(i, i ^ step) for i in range(workers)]
            sent = send(sent, swap, "worker")
        held.append(sent)
    spread = lax.all_to_all(
        mine[:, :cut], ("worker", "outer"), split_axis=0, concat_axis=0, tiled=True
    )
    first = (o % 2) == 0
    near = [jnp.where(first, tail, pair), jnp.where(first, pair, tail)]
    far = []
    for part in (tail, pair):
        crossed = send(part, ACROSS)
        far.append(jnp.where(is_end, send(crossed, TO_ENDS), crossed))
    low, high = near + far, far[::-1] + near
    line_v = jnp.stack([jnp.where(is_low, *parts) for parts in zip(low, high)])
    spread_v, share = center[:cut], 1 / worker_count

    places = jnp.stack([(w ^ step) * outers + o for step in steps])
    hit = places[:, None] == jnp.arange(worker_count)[None]

    def placed(line_sq):
        return jnp.sum(jnp.where(hit, line_sq[:, None], 0.0), axis=0)

    def factors(both):
        norm_sq = sum_over_devices(both)
        factor = jnp.minimum(1.0, radius_total * lax.rsqrt(norm_sq + epsilon))
        return factor, jnp.sum(jnp.where(hit, factor[None], 0.0), axis=1)

    line_sq, v = jnp.zeros((worker_count,), jnp.float32), line_v
    for place in reversed(range(workers)):
        square = jnp.sum(jnp.square(held[place] - v))
        line_sq = lax.optimization_barrier(line_sq + jnp.where(hit[place], square, 0.0))
        v = tie(v, line_sq)
    spread_sq = jnp.sum(jnp.square(spread - spread_v[None]), axis=(1, 2))
    factor, line_factor = factors(spread_sq + line_sq)

    flat = [value.reshape(outers * rest, columns) for value in held]
    flat_v = line_v.reshape(outers * rest, columns)
    end_flag = is_end.astype(jnp.int32).reshape(1)
    next_spread_v, spread_sq = move_spread(share, factor, spread, spread_v)
    early = {4: next_spread_v}
    count, places = len(sizes), begins(sizes)
    own = step_chunks(line_factor, flat, flat_v, 0, sizes[:1])
    own += step_chunks(line_factor, flat, tie(flat_v, own[0]), places[1], sizes[1:2])
    own += step_chunks(line_factor, flat, tie(flat_v, own[1]), places[2], sizes[2:4])
    own += step_chunks(line_factor, flat, tie(flat_v, own[2]), places[4], sizes[4:])
    cuts = [0, count - 5, count - 3, count - 1, count]
    groups = [slice(*pair) for pair in zip(cuts, cuts[1:])]
    totals, backs, carried = [], [], ()

    def move(part, carried):
        return move_chunks(
            end_flag, share, totals[part], backs[part], flat, flat_v,
            places[part.start], sizes[part], carried,
        )

    for chunk in range(count):
        got = send(own[chunk], TO_MIDS)
        if chunk >= 2:
            got = tie(got, totals[chunk - 2])
        total = own[chunk] + got
        total = total + send(total, ACROSS)
        if chunk in early:
            total = tie(total, early[chunk])
        if chunk in (count - 3, count - 1):
            carried = move(groups[chunk == count - 1], carried)
            total = tie(total, carried[1])
        totals.append(total)
        backs.append(send(total, TO_ENDS))
    for part in groups[2:]:
        carried = move(part, carried)
    spread_v = next_spread_v
    flat_v = carried[0]
    line_v = flat_v.reshape(line_v.shape)
    spread_sq = lax.optimization_barrier(jnp.sum(spread_sq, axis=(1, 2)))
    factor, line_factor = factors(spread_sq + placed(jnp.sum(carried[1], axis=(1, 2))))

    order = [jnp.where(is_low, LINE - 1 - place, place) for place in range(LINE)]
    block = step_blocks(order[:1], line_factor, held, line_v)
    block += step_blocks(order[1:], line_factor, held, tie(line_v, block[0]))
    arrived = [send(block[place], TO_MIDS) for place in range(3)]
    passed = [send(block[place] + arrived[place], ACROSS) for place in range(2)]
    end_sum = block[3] + send(block[3] + passed[0], TO_ENDS)
    mid_sum = block[2] + arrived[2] + passed[1]
    own_v = lax.dynamic_index_in_dim(line_v, o, 0, keepdims=False)
    own_v = own_v + jnp.where(is_end, end_sum, mid_sum) * share
    step = jnp.sum(factor[:, None, None] * (spread - spread_v[None]), axis=0)
    buffer = lax.optimization_barrier(jnp.pad(spread_v + step * share, ((0, rest), (0, 0))))
    return lax.dynamic_update_slice(buffer, own_v, (cut, 0))


def solution(mesh):
    in_specs = (P("worker", "outer", None, "mp"), P(("worker", "outer"), "mp"), P())
    out_specs = P(("worker", "outer"), "mp")

    return jax.shard_map(on_device, mesh=mesh, in_specs=in_specs, out_specs=out_specs, check_vma=False)
```

```python
import math

import jax
import jax.numpy as jnp
from jax import lax
from jax.experimental import pallas as pl
from jax.experimental.pallas import tpu as pltpu
from jax.sharding import PartitionSpec as P


D = 3584
ITERS = 2
KVW = 4096
AXES = ("worker", "outer", "mp")
LINE = 4
TILE = 8
SPREAD = 3 / 7

GRANT = 60 << 20

epsilon = 1e-06


def sum_over_devices(value):
    for axis in AXES:
        size = lax.axis_size(axis)
        step = 1
        while step < size:
            value = value + lax.ppermute(value, axis, [(i, i ^ step) for i in range(size)])
            step *= 2
    return value


def send(value, pairs, axis="outer"):
    return lax.ppermute(value, axis, pairs)


TO_MIDS = [(0, 1), (3, 2)]
ACROSS = [(1, 2), (2, 1)]
TO_ENDS = [(1, 0), (2, 3)]


def tie(value, earlier):
    return lax.optimization_barrier((value, earlier))[0]


def split(rows, outers):
    cut = int(rows * SPREAD) // TILE * TILE
    rest = rows - cut
    tiles = rest // TILE
    if outers != LINE or rest % TILE or tiles < 13 or not cut:
        return None
    sizes = [1] + [2] * ((tiles - 2) // 2) + [1] * (tiles % 2) + [1]
    return cut, sizes


SMEM = pl.BlockSpec(memory_space=pltpu.SMEM)


def run(kernel, grid, in_specs, out_specs, out_shape, operands, moved, aliases={}, prefetch=0):
    return pl.pallas_call(
        kernel,
        grid_spec=pltpu.PrefetchScalarGridSpec(
            num_scalar_prefetch=prefetch, grid=grid, in_specs=in_specs, out_specs=out_specs
        ),
        out_shape=out_shape,
        input_output_aliases=aliases,
        compiler_params=pltpu.CompilerParams(vmem_limit_bytes=GRANT),
        cost_estimate=pl.CostEstimate(flops=4 * moved, bytes_accessed=4 * moved, transcendentals=0),
    )(*operands)


def group_spec(begin, count, tile, columns):
    return pl.BlockSpec((tile, columns), lambda i: (jnp.clip(i - begin, 0, count - 1), 0))


def begins(sizes):
    return [sum(sizes[:i]) for i in range(len(sizes))]


def step_of(factor, values, v):
    return sum(factor[i] * (value[...] - v) for i, value in enumerate(values))


def step_chunks(factor, values, v, start, sizes):
    columns, tile, count = v.shape[1], TILE * LINE, len(values)
    places = begins(sizes)

    def kernel(factor, *refs):
        values, v, outs = refs[:count], refs[count], refs[count + 1 :]
        i = pl.program_id(0)
        total = step_of(factor, values, v[...])
        for out, begin, size in zip(outs, places, sizes):

            @pl.when((i >= begin) & (i < begin + size))
            def _(out=out):
                out[...] = total

    at = pl.BlockSpec((tile, columns), lambda i: (start + i, 0))
    outs = [group_spec(begin, size, tile, columns) for begin, size in zip(places, sizes)]
    shapes = [jax.ShapeDtypeStruct((size * tile, columns), v.dtype) for size in sizes]
    moved = (count + 2) * sum(sizes) * tile * columns
    in_specs = [SMEM] + [at] * (count + 1)
    return run(kernel, (sum(sizes),), in_specs, outs, shapes, (factor, *values, v), moved)


def move_chunks(is_end, share, totals, backs, values, v, start, sizes, carried):
    columns, tile, count, chunks = v.shape[1], TILE * LINE, len(values), len(sizes)
    places = begins(sizes)

    def kernel(is_end, v, *refs):
        values, rest = refs[:count], refs[count:]
        totals, backs, (v_out, sq_out) = rest[:chunks], rest[chunks : 2 * chunks], rest[-2:]
        i = pl.program_id(0)

        @pl.when(i == 0)
        def _():
            sq_out[...] = rest[-3][...] if carried else jnp.zeros_like(sq_out)

        for total, back, begin, size in zip(totals, backs, places, sizes):

            @pl.when((i >= begin) & (i < begin + size))
            def _(total=total, back=back):
                step = jnp.where(is_end[0] > 0, back[...], total[...])
                v_out[...] = v[...] + step * share

        moved = v_out[...]
        for k, value in enumerate(values):
            square = jnp.square(value[...] - moved)
            folded = sum(square[j : j + 8] for j in range(0, tile, 8))
            sq_out[k] += sum(folded[:, j : j + 128] for j in range(0, columns, 128))

    at = pl.BlockSpec((tile, columns), lambda i: (start + i, 0))
    squares = pl.BlockSpec((count, 8, 128), lambda i: (0, 0, 0))
    parts = [group_spec(begin, size, tile, columns) for begin, size in zip(places, sizes)]
    in_specs = [SMEM] + [at] * (count + 1) + parts + parts
    operands = (is_end, v, *values, *totals, *backs)
    aliases = {}
    if carried:
        in_specs += [pl.BlockSpec(memory_space=pl.ANY), squares]
        aliases = {len(operands): 0, len(operands) + 1: 1}
        operands += tuple(carried)
    shapes = (
        jax.ShapeDtypeStruct(v.shape, v.dtype),
        jax.ShapeDtypeStruct((count, 8, 128), v.dtype),
    )
    moved = (count + 4) * sum(sizes) * tile * columns
    return run(kernel, (sum(sizes),), in_specs, (at, squares), shapes, operands, moved, aliases)


def step_blocks(places, factor, values, v):
    _, rest, columns = v.shape
    count, blocks, parts = len(values), len(places), 4
    width = columns // parts

    def kernel(places, factor, *refs):
        values, v, outs = refs[:count], refs[count], refs[count + 1 :]
        total = step_of(factor, values, v[...])
        for k, out in enumerate(outs):

            @pl.when(pl.program_id(0) == k)
            def _(out=out):
                out[...] = total

    at = pl.BlockSpec((None, rest, width), lambda b, i, places: (places[b], 0, i))
    outs = [
        pl.BlockSpec(
            (rest, width), lambda b, i, _, k=k: (0, jnp.clip((b - k) * parts + i, 0, parts - 1))
        )
        for k in range(blocks)
    ]
    shapes = [jax.ShapeDtypeStruct((rest, columns), v.dtype)] * blocks
    moved = (count + 2) * blocks * rest * columns
    operands = (jnp.stack(places).astype(jnp.int32), factor, *values, v)
    in_specs = [SMEM] + [at] * (count + 1)
    return run(kernel, (blocks, parts), in_specs, outs, shapes, operands, moved, prefetch=1)


def move_spread(share, factor, values, v):
    (rows, columns), count = v.shape, values.shape[0]
    tile = 2 * TILE if rows % (2 * TILE) == 0 else TILE

    def kernel(factor, v, values, v_out, sq_out):
        base = v[...]
        moved = base + sum(factor[k] * (values[k] - base) for k in range(count)) * share
        v_out[...] = moved

        @pl.when(pl.program_id(0) == 0)
        def _():
            sq_out[...] = jnp.zeros_like(sq_out)

        for k in range(count):
            square = jnp.square(values[k] - moved)
            folded = sum(square[j : j + TILE] for j in range(0, tile, TILE))
            sq_out[k] += sum(folded[:, j : j + 128] for j in range(0, columns, 128))

    at = pl.BlockSpec((tile, columns), lambda i: (i, 0))
    stack = pl.BlockSpec((count, tile, columns), lambda i: (0, i, 0))
    squares = pl.BlockSpec((count, TILE, 128), lambda i: (0, 0, 0))
    shapes = (
        jax.ShapeDtypeStruct(v.shape, v.dtype),
        jax.ShapeDtypeStruct((count, TILE, 128), v.dtype),
    )
    moved = (count + 2) * rows * columns
    operands = (factor, v, values)
    return run(kernel, (rows // tile,), [SMEM, at, stack], (at, squares), shapes, operands, moved)


def spread_only(mine, center, radius_total, worker_count):
    own_rows = center
    gathered = lax.all_to_all(mine, ("worker", "outer"), split_axis=0, concat_axis=0, tiled=True)
    for _ in range(ITERS):
        difference = gathered - own_rows[None]
        norm_sq = sum_over_devices(jnp.sum(difference * difference, axis=(1, 2)))
        factor = jnp.minimum(1.0, radius_total * lax.rsqrt(norm_sq + epsilon))
        own_rows = own_rows + jnp.sum(factor[:, None, None] * difference, axis=0) / worker_count
    return own_rows


def on_device(grads, center, radius):
    workers, outers = lax.axis_size("worker"), lax.axis_size("outer")
    worker_count = workers * outers
    radius_total = radius[0] * math.sqrt(D * KVW)
    rows, columns = center.shape
    mine = grads.reshape(worker_count, rows, columns)
    plan = split(rows, outers)
    if plan is None:
        return spread_only(mine, center, radius_total, worker_count)
    cut, sizes = plan
    rest = rows - cut

    w, o = lax.axis_index("worker"), lax.axis_index("outer")
    is_end = (o == 0) | (o == LINE - 1)
    is_low = o < LINE // 2

    def line_rows(source, worker):
        return lax.dynamic_slice(source, (worker * outers, cut, 0), (outers, rest, columns))

    tail = center[cut:]
    pair = send(tail, [(i, i ^ 1) for i in range(LINE)])
    steps = list(range(workers // 2, workers)) + list(range(1, workers // 2)) + [0]
    held, source = [], mine
    for step in steps:
        sent = line_rows(source, w ^ step)
        source = tie(source, sent)
        if step:
            swap = [(i, i ^ step) for i in range(workers)]
            sent = send(sent, swap, "worker")
        held.append(sent)
    spread = lax.all_to_all(
        mine[:, :cut], ("worker", "outer"), split_axis=0, concat_axis=0, tiled=True
    )
    first = (o % 2) == 0
    near = [jnp.where(first, tail, pair), jnp.where(first, pair, tail)]
    far = []
    for part in (tail, pair):
        crossed = send(part, ACROSS)
        far.append(jnp.where(is_end, send(crossed, TO_ENDS), crossed))
    low, high = near + far, far[::-1] + near
    line_v = jnp.stack([jnp.where(is_low, *parts) for parts in zip(low, high)])
    spread_v, share = center[:cut], 1 / worker_count

    places = jnp.stack([(w ^ step) * outers + o for step in steps])
    hit = places[:, None] == jnp.arange(worker_count)[None]

    def placed(line_sq):
        return jnp.sum(jnp.where(hit, line_sq[:, None], 0.0), axis=0)

    def factors(both):
        norm_sq = sum_over_devices(both)
        factor = jnp.minimum(1.0, radius_total * lax.rsqrt(norm_sq + epsilon))
        return factor, jnp.sum(jnp.where(hit, factor[None], 0.0), axis=1)

    line_sq, v = jnp.zeros((worker_count,), jnp.float32), line_v
    for place in reversed(range(workers)):
        square = jnp.sum(jnp.square(held[place] - v))
        line_sq = lax.optimization_barrier(line_sq + jnp.where(hit[place], square, 0.0))
        v = tie(v, line_sq)
    spread_sq = jnp.sum(jnp.square(spread - spread_v[None]), axis=(1, 2))
    factor, line_factor = factors(spread_sq + line_sq)

    flat = [value.reshape(outers * rest, columns) for value in held]
    flat_v = line_v.reshape(outers * rest, columns)
    end_flag = is_end.astype(jnp.int32).reshape(1)
    next_spread_v, spread_sq = move_spread(share, factor, spread, spread_v)
    early = {2: next_spread_v}
    count, places = len(sizes), begins(sizes)
    own = step_chunks(line_factor, flat, flat_v, 0, sizes[:1])
    own += step_chunks(line_factor, flat, tie(flat_v, own[0]), places[1], sizes[1:2])
    own += step_chunks(line_factor, flat, tie(flat_v, own[1]), places[2], sizes[2:4])
    own += step_chunks(line_factor, flat, tie(flat_v, own[2]), places[4], sizes[4:])
    cuts = [0, count - 5, count - 3, count - 1, count]
    groups = [slice(*pair) for pair in zip(cuts, cuts[1:])]
    totals, backs, carried = [], [], ()

    def move(part, carried):
        return move_chunks(
            end_flag, share, totals[part], backs[part], flat, flat_v,
            places[part.start], sizes[part], carried,
        )

    for chunk in range(count):
        got = send(own[chunk], TO_MIDS)
        if chunk >= 2:
            got = tie(got, totals[chunk - 2])
        total = own[chunk] + got
        total = total + send(total, ACROSS)
        if chunk in early:
            total = tie(total, early[chunk])
        totals.append(total)
        backs.append(send(total, TO_ENDS))
    carried = move(groups[0], carried)
    for part in groups[1:]:
        carried = move(part, carried)
    spread_v = next_spread_v
    flat_v = carried[0]
    line_v = flat_v.reshape(line_v.shape)
    spread_sq = lax.optimization_barrier(jnp.sum(spread_sq, axis=(1, 2)))
    factor, line_factor = factors(spread_sq + placed(jnp.sum(carried[1], axis=(1, 2))))

    order = [jnp.where(is_low, LINE - 1 - place, place) for place in range(LINE)]
    block = step_blocks(order[:1], line_factor, held, line_v)
    block += step_blocks(order[1:], line_factor, held, tie(line_v, block[0]))
    arrived = [send(block[place], TO_MIDS) for place in range(3)]
    passed = [send(block[place] + arrived[place], ACROSS) for place in range(2)]
    end_sum = block[3] + send(block[3] + passed[0], TO_ENDS)
    mid_sum = block[2] + arrived[2] + passed[1]
    own_v = lax.dynamic_index_in_dim(line_v, o, 0, keepdims=False)
    own_v = own_v + jnp.where(is_end, end_sum, mid_sum) * share
    step = jnp.sum(factor[:, None, None] * (spread - spread_v[None]), axis=0)
    buffer = lax.optimization_barrier(jnp.pad(spread_v + step * share, ((0, rest), (0, 0))))
    return lax.dynamic_update_slice(buffer, own_v, (cut, 0))


def solution(mesh):
    in_specs = (P("worker", "outer", None, "mp"), P(("worker", "outer"), "mp"), P())
    out_specs = P(("worker", "outer"), "mp")

    return jax.shard_map(on_device, mesh=mesh, in_specs=in_specs, out_specs=out_specs, check_vma=False)
```

```python
import math

import jax
import jax.numpy as jnp
from jax import lax
from jax.experimental import pallas as pl
from jax.experimental.pallas import tpu as pltpu
from jax.sharding import PartitionSpec as P


D = 3584
ITERS = 2
KVW = 4096
AXES = ("worker", "outer", "mp")
LINE = 4
TILE = 8
SPREAD = 3 / 7

GRANT = 60 << 20

epsilon = 1e-06


def sum_over_devices(value):
    for axis in AXES:
        size = lax.axis_size(axis)
        step = 1
        while step < size:
            value = value + lax.ppermute(value, axis, [(i, i ^ step) for i in range(size)])
            step *= 2
    return value


def send(value, pairs, axis="outer"):
    return lax.ppermute(value, axis, pairs)


TO_MIDS = [(0, 1), (3, 2)]
ACROSS = [(1, 2), (2, 1)]
TO_ENDS = [(1, 0), (2, 3)]


def tie(value, earlier):
    return lax.optimization_barrier((value, earlier))[0]


def split(rows, outers):
    cut = int(rows * SPREAD) // TILE * TILE
    rest = rows - cut
    tiles = rest // TILE
    if outers != LINE or rest % TILE or tiles < 13 or not cut:
        return None
    sizes = [1] + [2] * ((tiles - 2) // 2) + [1] * (tiles % 2) + [1]
    return cut, sizes


SMEM = pl.BlockSpec(memory_space=pltpu.SMEM)


def run(kernel, grid, in_specs, out_specs, out_shape, operands, moved, aliases={}, prefetch=0):
    return pl.pallas_call(
        kernel,
        grid_spec=pltpu.PrefetchScalarGridSpec(
            num_scalar_prefetch=prefetch, grid=grid, in_specs=in_specs, out_specs=out_specs
        ),
        out_shape=out_shape,
        input_output_aliases=aliases,
        compiler_params=pltpu.CompilerParams(vmem_limit_bytes=GRANT),
        cost_estimate=pl.CostEstimate(flops=4 * moved, bytes_accessed=4 * moved, transcendentals=0),
    )(*operands)


def group_spec(begin, count, tile, columns):
    return pl.BlockSpec((tile, columns), lambda i: (jnp.clip(i - begin, 0, count - 1), 0))


def begins(sizes):
    return [sum(sizes[:i]) for i in range(len(sizes))]


def step_of(factor, values, v):
    return sum(factor[i] * (value[...] - v) for i, value in enumerate(values))


def step_chunks(factor, values, v, start, sizes):
    columns, tile, count = v.shape[1], TILE * LINE, len(values)
    places = begins(sizes)

    def kernel(factor, *refs):
        values, v, outs = refs[:count], refs[count], refs[count + 1 :]
        i = pl.program_id(0)
        total = step_of(factor, values, v[...])
        for out, begin, size in zip(outs, places, sizes):

            @pl.when((i >= begin) & (i < begin + size))
            def _(out=out):
                out[...] = total

    at = pl.BlockSpec((tile, columns), lambda i: (start + i, 0))
    outs = [group_spec(begin, size, tile, columns) for begin, size in zip(places, sizes)]
    shapes = [jax.ShapeDtypeStruct((size * tile, columns), v.dtype) for size in sizes]
    moved = (count + 2) * sum(sizes) * tile * columns
    in_specs = [SMEM] + [at] * (count + 1)
    return run(kernel, (sum(sizes),), in_specs, outs, shapes, (factor, *values, v), moved)


def move_chunks(is_end, share, totals, backs, values, v, start, sizes, carried):
    columns, tile, count, chunks = v.shape[1], TILE * LINE, len(values), len(sizes)
    places = begins(sizes)

    def kernel(is_end, v, *refs):
        values, rest = refs[:count], refs[count:]
        totals, backs, (v_out, sq_out) = rest[:chunks], rest[chunks : 2 * chunks], rest[-2:]
        i = pl.program_id(0)

        @pl.when(i == 0)
        def _():
            sq_out[...] = rest[-3][...] if carried else jnp.zeros_like(sq_out)

        for total, back, begin, size in zip(totals, backs, places, sizes):

            @pl.when((i >= begin) & (i < begin + size))
            def _(total=total, back=back):
                step = jnp.where(is_end[0] > 0, back[...], total[...])
                v_out[...] = v[...] + step * share

        moved = v_out[...]
        for k, value in enumerate(values):
            square = jnp.square(value[...] - moved)
            folded = sum(square[j : j + 8] for j in range(0, tile, 8))
            sq_out[k] += sum(folded[:, j : j + 128] for j in range(0, columns, 128))

    at = pl.BlockSpec((tile, columns), lambda i: (start + i, 0))
    squares = pl.BlockSpec((count, 8, 128), lambda i: (0, 0, 0))
    parts = [group_spec(begin, size, tile, columns) for begin, size in zip(places, sizes)]
    in_specs = [SMEM] + [at] * (count + 1) + parts + parts
    operands = (is_end, v, *values, *totals, *backs)
    aliases = {}
    if carried:
        in_specs += [pl.BlockSpec(memory_space=pl.ANY), squares]
        aliases = {len(operands): 0, len(operands) + 1: 1}
        operands += tuple(carried)
    shapes = (
        jax.ShapeDtypeStruct(v.shape, v.dtype),
        jax.ShapeDtypeStruct((count, 8, 128), v.dtype),
    )
    moved = (count + 4) * sum(sizes) * tile * columns
    return run(kernel, (sum(sizes),), in_specs, (at, squares), shapes, operands, moved, aliases)


def step_blocks(places, factor, values, v):
    _, rest, columns = v.shape
    count, blocks, parts = len(values), len(places), 4
    width = columns // parts

    def kernel(places, factor, *refs):
        values, v, outs = refs[:count], refs[count], refs[count + 1 :]
        total = step_of(factor, values, v[...])
        for k, out in enumerate(outs):

            @pl.when(pl.program_id(0) == k)
            def _(out=out):
                out[...] = total

    at = pl.BlockSpec((None, rest, width), lambda b, i, places: (places[b], 0, i))
    outs = [
        pl.BlockSpec(
            (rest, width), lambda b, i, _, k=k: (0, jnp.clip((b - k) * parts + i, 0, parts - 1))
        )
        for k in range(blocks)
    ]
    shapes = [jax.ShapeDtypeStruct((rest, columns), v.dtype)] * blocks
    moved = (count + 2) * blocks * rest * columns
    operands = (jnp.stack(places).astype(jnp.int32), factor, *values, v)
    in_specs = [SMEM] + [at] * (count + 1)
    return run(kernel, (blocks, parts), in_specs, outs, shapes, operands, moved, prefetch=1)


def move_spread(share, factor, values, v):
    (rows, columns), count = v.shape, values.shape[0]
    tile = 2 * TILE if rows % (2 * TILE) == 0 else TILE

    def kernel(factor, v, values, v_out, sq_out):
        base = v[...]
        moved = base + sum(factor[k] * (values[k] - base) for k in range(count)) * share
        v_out[...] = moved

        @pl.when(pl.program_id(0) == 0)
        def _():
            sq_out[...] = jnp.zeros_like(sq_out)

        for k in range(count):
            square = jnp.square(values[k] - moved)
            folded = sum(square[j : j + TILE] for j in range(0, tile, TILE))
            sq_out[k] += sum(folded[:, j : j + 128] for j in range(0, columns, 128))

    at = pl.BlockSpec((tile, columns), lambda i: (i, 0))
    stack = pl.BlockSpec((count, tile, columns), lambda i: (0, i, 0))
    squares = pl.BlockSpec((count, TILE, 128), lambda i: (0, 0, 0))
    shapes = (
        jax.ShapeDtypeStruct(v.shape, v.dtype),
        jax.ShapeDtypeStruct((count, TILE, 128), v.dtype),
    )
    moved = (count + 2) * rows * columns
    operands = (factor, v, values)
    return run(kernel, (rows // tile,), [SMEM, at, stack], (at, squares), shapes, operands, moved)


def spread_only(mine, center, radius_total, worker_count):
    own_rows = center
    gathered = lax.all_to_all(mine, ("worker", "outer"), split_axis=0, concat_axis=0, tiled=True)
    for _ in range(ITERS):
        difference = gathered - own_rows[None]
        norm_sq = sum_over_devices(jnp.sum(difference * difference, axis=(1, 2)))
        factor = jnp.minimum(1.0, radius_total * lax.rsqrt(norm_sq + epsilon))
        own_rows = own_rows + jnp.sum(factor[:, None, None] * difference, axis=0) / worker_count
    return own_rows


def on_device(grads, center, radius):
    workers, outers = lax.axis_size("worker"), lax.axis_size("outer")
    worker_count = workers * outers
    radius_total = radius[0] * math.sqrt(D * KVW)
    rows, columns = center.shape
    mine = grads.reshape(worker_count, rows, columns)
    plan = split(rows, outers)
    if plan is None:
        return spread_only(mine, center, radius_total, worker_count)
    cut, sizes = plan
    rest = rows - cut

    w, o = lax.axis_index("worker"), lax.axis_index("outer")
    is_end = (o == 0) | (o == LINE - 1)
    is_low = o < LINE // 2

    def line_rows(source, worker):
        return lax.dynamic_slice(source, (worker * outers, cut, 0), (outers, rest, columns))

    tail = center[cut:]
    pair = send(tail, [(i, i ^ 1) for i in range(LINE)])
    steps = list(range(workers // 2, workers)) + list(range(1, workers // 2)) + [0]
    held, source = [], mine
    for step in steps:
        sent = line_rows(source, w ^ step)
        source = tie(source, sent)
        if step:
            swap = [(i, i ^ step) for i in range(workers)]
            sent = send(sent, swap, "worker")
        held.append(sent)
    spread = lax.all_to_all(
        mine[:, :cut], ("worker", "outer"), split_axis=0, concat_axis=0, tiled=True
    )
    first = (o % 2) == 0
    near = [jnp.where(first, tail, pair), jnp.where(first, pair, tail)]
    far = []
    for part in (tail, pair):
        crossed = send(part, ACROSS)
        far.append(jnp.where(is_end, send(crossed, TO_ENDS), crossed))
    low, high = near + far, far[::-1] + near
    line_v = jnp.stack([jnp.where(is_low, *parts) for parts in zip(low, high)])
    spread_v, share = center[:cut], 1 / worker_count

    places = jnp.stack([(w ^ step) * outers + o for step in steps])
    hit = places[:, None] == jnp.arange(worker_count)[None]

    def placed(line_sq):
        return jnp.sum(jnp.where(hit, line_sq[:, None], 0.0), axis=0)

    def factors(both):
        norm_sq = sum_over_devices(both)
        factor = jnp.minimum(1.0, radius_total * lax.rsqrt(norm_sq + epsilon))
        return factor, jnp.sum(jnp.where(hit, factor[None], 0.0), axis=1)

    line_sq, v = jnp.zeros((worker_count,), jnp.float32), line_v
    for place in reversed(range(workers)):
        square = jnp.sum(jnp.square(held[place] - v))
        line_sq = lax.optimization_barrier(line_sq + jnp.where(hit[place], square, 0.0))
        v = tie(v, line_sq)
    spread_sq = jnp.sum(jnp.square(spread - spread_v[None]), axis=(1, 2))
    factor, line_factor = factors(spread_sq + line_sq)

    flat = [value.reshape(outers * rest, columns) for value in held]
    flat_v = line_v.reshape(outers * rest, columns)
    end_flag = is_end.astype(jnp.int32).reshape(1)
    next_spread_v, spread_sq = move_spread(share, factor, spread, spread_v)
    early = {4: next_spread_v}
    count, places = len(sizes), begins(sizes)
    own = step_chunks(line_factor, flat, flat_v, 0, sizes[:1])
    own += step_chunks(line_factor, flat, tie(flat_v, own[0]), places[1], sizes[1:2])
    own += step_chunks(line_factor, flat, tie(flat_v, own[1]), places[2], sizes[2:4])
    own += step_chunks(line_factor, flat, tie(flat_v, own[2]), places[4], sizes[4:6])
    own += step_chunks(line_factor, flat, tie(flat_v, own[4]), places[6], sizes[6:])
    cuts = [0, count - 6, count - 4, count - 2, count]
    groups = [slice(*pair) for pair in zip(cuts, cuts[1:])]
    totals, backs, carried = [], [], ()

    def move(part, carried):
        return move_chunks(
            end_flag, share, totals[part], backs[part], flat, flat_v,
            places[part.start], sizes[part], carried,
        )

    for chunk in range(count):
        got = send(own[chunk], TO_MIDS)
        if chunk >= 2:
            got = tie(got, totals[chunk - 2])
        total = own[chunk] + got
        total = total + send(total, ACROSS)
        if chunk in early:
            total = tie(total, early[chunk])
        if chunk == count - 3:
            carried = move(groups[0], carried)
            total = tie(total, carried[1])
        totals.append(total)
        backs.append(send(total, TO_ENDS))
    carried = move(groups[1], carried)
    for part in groups[2:]:
        carried = move(part, carried)
    spread_v = next_spread_v
    flat_v = carried[0]
    line_v = flat_v.reshape(line_v.shape)
    spread_sq = lax.optimization_barrier(jnp.sum(spread_sq, axis=(1, 2)))
    factor, line_factor = factors(spread_sq + placed(jnp.sum(carried[1], axis=(1, 2))))

    order = [jnp.where(is_low, LINE - 1 - place, place) for place in range(LINE)]
    block = step_blocks(order[:1], line_factor, held, line_v)
    block += step_blocks(order[1:], line_factor, held, tie(line_v, block[0]))
    arrived = [send(block[place], TO_MIDS) for place in range(3)]
    passed = [send(block[place] + arrived[place], ACROSS) for place in range(2)]
    end_sum = block[3] + send(block[3] + passed[0], TO_ENDS)
    mid_sum = block[2] + arrived[2] + passed[1]
    own_v = lax.dynamic_index_in_dim(line_v, o, 0, keepdims=False)
    own_v = own_v + jnp.where(is_end, end_sum, mid_sum) * share
    step = jnp.sum(factor[:, None, None] * (spread - spread_v[None]), axis=0)
    buffer = lax.optimization_barrier(jnp.pad(spread_v + step * share, ((0, rest), (0, 0))))
    return lax.dynamic_update_slice(buffer, own_v, (cut, 0))


def solution(mesh):
    in_specs = (P("worker", "outer", None, "mp"), P(("worker", "outer"), "mp"), P())
    out_specs = P(("worker", "outer"), "mp")

    return jax.shard_map(on_device, mesh=mesh, in_specs=in_specs, out_specs=out_specs, check_vma=False)
```

```python
import math

import jax
import jax.numpy as jnp
from jax import lax
from jax.experimental import pallas as pl
from jax.experimental.pallas import tpu as pltpu
from jax.sharding import PartitionSpec as P


D = 3584
ITERS = 2
KVW = 4096
AXES = ("worker", "outer", "mp")
LINE = 4
TILE = 8
UNIT = 16
SPREAD = 3 / 7

GRANT = 60 << 20

epsilon = 1e-06


def sum_over_devices(value):
    for axis in AXES:
        size = lax.axis_size(axis)
        step = 1
        while step < size:
            value = value + lax.ppermute(value, axis, [(i, i ^ step) for i in range(size)])
            step *= 2
    return value


def send(value, pairs, axis="outer"):
    return lax.ppermute(value, axis, pairs)


TO_MIDS = [(0, 1), (3, 2)]
ACROSS = [(1, 2), (2, 1)]
TO_ENDS = [(1, 0), (2, 3)]


def tie(value, earlier):
    return lax.optimization_barrier((value, earlier))[0]


def split(rows, outers):
    cut = int(rows * SPREAD) // TILE * TILE
    rest = rows - cut
    units = rest * outers // UNIT
    if outers != LINE or rest % TILE or units < 22 or not cut:
        return None
    body = units - 7
    sizes = [3] + [5] * (body // 5) + [body % 5] * (body % 5 > 0) + [4]
    return cut, sizes


SMEM = pl.BlockSpec(memory_space=pltpu.SMEM)


def run(kernel, grid, in_specs, out_specs, out_shape, operands, moved, aliases={}, prefetch=0):
    return pl.pallas_call(
        kernel,
        grid_spec=pltpu.PrefetchScalarGridSpec(
            num_scalar_prefetch=prefetch, grid=grid, in_specs=in_specs, out_specs=out_specs
        ),
        out_shape=out_shape,
        input_output_aliases=aliases,
        compiler_params=pltpu.CompilerParams(vmem_limit_bytes=GRANT),
        cost_estimate=pl.CostEstimate(flops=4 * moved, bytes_accessed=4 * moved, transcendentals=0),
    )(*operands)


def group_spec(begin, count, tile, columns):
    return pl.BlockSpec((tile, columns), lambda i: (jnp.clip(i - begin, 0, count - 1), 0))


def begins(sizes):
    return [sum(sizes[:i]) for i in range(len(sizes))]


def step_of(factor, values, v):
    return sum(factor[i] * (value[...] - v) for i, value in enumerate(values))


def step_chunks(factor, values, v, start, sizes):
    columns, tile, count = v.shape[1], UNIT, len(values)
    places = begins(sizes)

    def kernel(factor, *refs):
        values, v, outs = refs[:count], refs[count], refs[count + 1 :]
        i = pl.program_id(0)
        total = step_of(factor, values, v[...])
        for out, begin, size in zip(outs, places, sizes):

            @pl.when((i >= begin) & (i < begin + size))
            def _(out=out):
                out[...] = total

    at = pl.BlockSpec((tile, columns), lambda i: (start + i, 0))
    outs = [group_spec(begin, size, tile, columns) for begin, size in zip(places, sizes)]
    shapes = [jax.ShapeDtypeStruct((size * tile, columns), v.dtype) for size in sizes]
    moved = (count + 2) * sum(sizes) * tile * columns
    in_specs = [SMEM] + [at] * (count + 1)
    return run(kernel, (sum(sizes),), in_specs, outs, shapes, (factor, *values, v), moved)


def move_chunks(is_end, share, totals, backs, values, v, start, sizes, carried):
    columns, tile, count, chunks = v.shape[1], UNIT, len(values), len(sizes)
    places = begins(sizes)

    def kernel(is_end, v, *refs):
        values, rest = refs[:count], refs[count:]
        totals, backs, (v_out, sq_out) = rest[:chunks], rest[chunks : 2 * chunks], rest[-2:]
        i = pl.program_id(0)

        @pl.when(i == 0)
        def _():
            sq_out[...] = rest[-3][...] if carried else jnp.zeros_like(sq_out)

        for total, back, begin, size in zip(totals, backs, places, sizes):

            @pl.when((i >= begin) & (i < begin + size))
            def _(total=total, back=back):
                step = jnp.where(is_end[0] > 0, back[...], total[...])
                v_out[...] = v[...] + step * share

        moved = v_out[...]
        for k, value in enumerate(values):
            square = jnp.square(value[...] - moved)
            folded = sum(square[j : j + 8] for j in range(0, tile, 8))
            sq_out[k] += sum(folded[:, j : j + 128] for j in range(0, columns, 128))

    at = pl.BlockSpec((tile, columns), lambda i: (start + i, 0))
    squares = pl.BlockSpec((count, 8, 128), lambda i: (0, 0, 0))
    parts = [group_spec(begin, size, tile, columns) for begin, size in zip(places, sizes)]
    in_specs = [SMEM] + [at] * (count + 1) + parts + parts
    operands = (is_end, v, *values, *totals, *backs)
    aliases = {}
    if carried:
        in_specs += [pl.BlockSpec(memory_space=pl.ANY), squares]
        aliases = {len(operands): 0, len(operands) + 1: 1}
        operands += tuple(carried)
    shapes = (
        jax.ShapeDtypeStruct(v.shape, v.dtype),
        jax.ShapeDtypeStruct((count, 8, 128), v.dtype),
    )
    moved = (count + 4) * sum(sizes) * tile * columns
    return run(kernel, (sum(sizes),), in_specs, (at, squares), shapes, operands, moved, aliases)


def step_blocks(places, factor, values, v):
    _, rest, columns = v.shape
    count, blocks, parts = len(values), len(places), 4
    width = columns // parts

    def kernel(places, factor, *refs):
        values, v, outs = refs[:count], refs[count], refs[count + 1 :]
        total = step_of(factor, values, v[...])
        for k, out in enumerate(outs):

            @pl.when(pl.program_id(0) == k)
            def _(out=out):
                out[...] = total

    at = pl.BlockSpec((None, rest, width), lambda b, i, places: (places[b], 0, i))
    outs = [
        pl.BlockSpec(
            (rest, width), lambda b, i, _, k=k: (0, jnp.clip((b - k) * parts + i, 0, parts - 1))
        )
        for k in range(blocks)
    ]
    shapes = [jax.ShapeDtypeStruct((rest, columns), v.dtype)] * blocks
    moved = (count + 2) * blocks * rest * columns
    operands = (jnp.stack(places).astype(jnp.int32), factor, *values, v)
    in_specs = [SMEM] + [at] * (count + 1)
    return run(kernel, (blocks, parts), in_specs, outs, shapes, operands, moved, prefetch=1)


def move_spread(share, factor, values, v):
    (rows, columns), count = v.shape, values.shape[0]
    tile = 2 * TILE if rows % (2 * TILE) == 0 else TILE

    def kernel(factor, v, values, v_out, sq_out):
        base = v[...]
        moved = base + sum(factor[k] * (values[k] - base) for k in range(count)) * share
        v_out[...] = moved

        @pl.when(pl.program_id(0) == 0)
        def _():
            sq_out[...] = jnp.zeros_like(sq_out)

        for k in range(count):
            square = jnp.square(values[k] - moved)
            folded = sum(square[j : j + TILE] for j in range(0, tile, TILE))
            sq_out[k] += sum(folded[:, j : j + 128] for j in range(0, columns, 128))

    at = pl.BlockSpec((tile, columns), lambda i: (i, 0))
    stack = pl.BlockSpec((count, tile, columns), lambda i: (0, i, 0))
    squares = pl.BlockSpec((count, TILE, 128), lambda i: (0, 0, 0))
    shapes = (
        jax.ShapeDtypeStruct(v.shape, v.dtype),
        jax.ShapeDtypeStruct((count, TILE, 128), v.dtype),
    )
    moved = (count + 2) * rows * columns
    operands = (factor, v, values)
    return run(kernel, (rows // tile,), [SMEM, at, stack], (at, squares), shapes, operands, moved)


def spread_only(mine, center, radius_total, worker_count):
    own_rows = center
    gathered = lax.all_to_all(mine, ("worker", "outer"), split_axis=0, concat_axis=0, tiled=True)
    for _ in range(ITERS):
        difference = gathered - own_rows[None]
        norm_sq = sum_over_devices(jnp.sum(difference * difference, axis=(1, 2)))
        factor = jnp.minimum(1.0, radius_total * lax.rsqrt(norm_sq + epsilon))
        own_rows = own_rows + jnp.sum(factor[:, None, None] * difference, axis=0) / worker_count
    return own_rows


def on_device(grads, center, radius):
    workers, outers = lax.axis_size("worker"), lax.axis_size("outer")
    worker_count = workers * outers
    radius_total = radius[0] * math.sqrt(D * KVW)
    rows, columns = center.shape
    mine = grads.reshape(worker_count, rows, columns)
    plan = split(rows, outers)
    if plan is None:
        return spread_only(mine, center, radius_total, worker_count)
    cut, sizes = plan
    rest = rows - cut

    w, o = lax.axis_index("worker"), lax.axis_index("outer")
    is_end = (o == 0) | (o == LINE - 1)
    is_low = o < LINE // 2

    def line_rows(source, worker):
        return lax.dynamic_slice(source, (worker * outers, cut, 0), (outers, rest, columns))

    tail = center[cut:]
    pair = send(tail, [(i, i ^ 1) for i in range(LINE)])
    steps = list(range(workers // 2, workers)) + list(range(1, workers // 2)) + [0]
    held, source = [], mine
    for step in steps:
        sent = line_rows(source, w ^ step)
        source = tie(source, sent)
        if step:
            swap = [(i, i ^ step) for i in range(workers)]
            sent = send(sent, swap, "worker")
        held.append(sent)
    spread = lax.all_to_all(
        mine[:, :cut], ("worker", "outer"), split_axis=0, concat_axis=0, tiled=True
    )
    first = (o % 2) == 0
    near = [jnp.where(first, tail, pair), jnp.where(first, pair, tail)]
    far = []
    for part in (tail, pair):
        crossed = send(part, ACROSS)
        far.append(jnp.where(is_end, send(crossed, TO_ENDS), crossed))
    low, high = near + far, far[::-1] + near
    line_v = jnp.stack([jnp.where(is_low, *parts) for parts in zip(low, high)])
    spread_v, share = center[:cut], 1 / worker_count

    places = jnp.stack([(w ^ step) * outers + o for step in steps])
    hit = places[:, None] == jnp.arange(worker_count)[None]

    def placed(line_sq):
        return jnp.sum(jnp.where(hit, line_sq[:, None], 0.0), axis=0)

    def factors(both):
        norm_sq = sum_over_devices(both)
        factor = jnp.minimum(1.0, radius_total * lax.rsqrt(norm_sq + epsilon))
        return factor, jnp.sum(jnp.where(hit, factor[None], 0.0), axis=1)

    line_sq, v = jnp.zeros((worker_count,), jnp.float32), line_v
    for place in reversed(range(workers)):
        square = jnp.sum(jnp.square(held[place] - v))
        line_sq = lax.optimization_barrier(line_sq + jnp.where(hit[place], square, 0.0))
        v = tie(v, line_sq)
    spread_sq = jnp.sum(jnp.square(spread - spread_v[None]), axis=(1, 2))
    factor, line_factor = factors(spread_sq + line_sq)

    flat = [value.reshape(outers * rest, columns) for value in held]
    flat_v = line_v.reshape(outers * rest, columns)
    end_flag = is_end.astype(jnp.int32).reshape(1)
    next_spread_v, spread_sq = move_spread(share, factor, spread, spread_v)
    early = {3: next_spread_v}
    count, places = len(sizes), begins(sizes)
    own = step_chunks(line_factor, flat, flat_v, 0, sizes[:1])
    own += step_chunks(line_factor, flat, tie(flat_v, own[0]), places[1], sizes[1:2])
    own += step_chunks(line_factor, flat, tie(flat_v, own[1]), places[2], sizes[2:4])
    own += step_chunks(line_factor, flat, tie(flat_v, own[2]), places[4], sizes[4:])
    cuts = [0, count - 5, count - 3, count - 1, count]
    groups = [slice(*pair) for pair in zip(cuts, cuts[1:])]
    totals, backs, carried = [], [], ()

    def move(part, carried):
        return move_chunks(
            end_flag, share, totals[part], backs[part], flat, flat_v,
            places[part.start], sizes[part], carried,
        )

    for chunk in range(count):
        got = send(own[chunk], TO_MIDS)
        if chunk >= 2:
            got = tie(got, totals[chunk - 2])
        total = own[chunk] + got
        total = total + send(total, ACROSS)
        if chunk in early:
            total = tie(total, early[chunk])
        if chunk == count - 2:
            carried = move(groups[0], carried)
            total = tie(total, carried[1])
        totals.append(total)
        backs.append(send(total, TO_ENDS))
    carried = move(groups[1], carried)
    for part in groups[2:]:
        carried = move(part, carried)
    spread_v = next_spread_v
    flat_v = carried[0]
    line_v = flat_v.reshape(line_v.shape)
    spread_sq = lax.optimization_barrier(jnp.sum(spread_sq, axis=(1, 2)))
    factor, line_factor = factors(spread_sq + placed(jnp.sum(carried[1], axis=(1, 2))))

    order = [jnp.where(is_low, LINE - 1 - place, place) for place in range(LINE)]
    block = step_blocks(order[:1], line_factor, held, line_v)
    block += step_blocks(order[1:], line_factor, held, tie(line_v, block[0]))
    arrived = [send(block[place], TO_MIDS) for place in range(3)]
    passed = [send(block[place] + arrived[place], ACROSS) for place in range(2)]
    end_sum = block[3] + send(block[3] + passed[0], TO_ENDS)
    mid_sum = block[2] + arrived[2] + passed[1]
    own_v = lax.dynamic_index_in_dim(line_v, o, 0, keepdims=False)
    own_v = own_v + jnp.where(is_end, end_sum, mid_sum) * share
    step = jnp.sum(factor[:, None, None] * (spread - spread_v[None]), axis=0)
    buffer = lax.optimization_barrier(jnp.pad(spread_v + step * share, ((0, rest), (0, 0))))
    return lax.dynamic_update_slice(buffer, own_v, (cut, 0))


def solution(mesh):
    in_specs = (P("worker", "outer", None, "mp"), P(("worker", "outer"), "mp"), P())
    out_specs = P(("worker", "outer"), "mp")

    return jax.shard_map(on_device, mesh=mesh, in_specs=in_specs, out_specs=out_specs, check_vma=False)
```

```python
import math

import jax
import jax.numpy as jnp
from jax import lax
from jax.experimental import pallas as pl
from jax.experimental.pallas import tpu as pltpu
from jax.sharding import PartitionSpec as P


D = 3584
ITERS = 2
KVW = 4096
AXES = ("worker", "outer", "mp")
LINE = 4
TILE = 8
UNIT = 16
SPREAD = 3 / 7

GRANT = 8 << 20

epsilon = 1e-06


def sum_over_devices(value):
    for axis in AXES:
        size = lax.axis_size(axis)
        step = 1
        while step < size:
            value = value + lax.ppermute(value, axis, [(i, i ^ step) for i in range(size)])
            step *= 2
    return value


def send(value, pairs, axis="outer"):
    return lax.ppermute(value, axis, pairs)


TO_MIDS = [(0, 1), (3, 2)]
ACROSS = [(1, 2), (2, 1)]
TO_ENDS = [(1, 0), (2, 3)]


def tie(value, earlier):
    return lax.optimization_barrier((value, earlier))[0]


def split(rows, outers):
    cut = int(rows * SPREAD) // TILE * TILE
    rest = rows - cut
    units = rest * outers // UNIT
    if outers != LINE or rest % TILE or units < 22 or not cut:
        return None
    body = units - 12
    sizes = [2, 4] + [5] * (body // 5) + [body % 5] * (body % 5 > 0) + [4, 2]
    return cut, sizes


SMEM = pl.BlockSpec(memory_space=pltpu.SMEM)


def run(kernel, grid, in_specs, out_specs, out_shape, operands, moved, aliases={}, prefetch=0):
    return pl.pallas_call(
        kernel,
        grid_spec=pltpu.PrefetchScalarGridSpec(
            num_scalar_prefetch=prefetch, grid=grid, in_specs=in_specs, out_specs=out_specs
        ),
        out_shape=out_shape,
        input_output_aliases=aliases,
        compiler_params=pltpu.CompilerParams(vmem_limit_bytes=GRANT),
        cost_estimate=pl.CostEstimate(flops=4 * moved, bytes_accessed=4 * moved, transcendentals=0),
    )(*operands)


def group_spec(begin, count, tile, columns):
    return pl.BlockSpec((tile, columns), lambda i: (jnp.clip(i - begin, 0, count - 1), 0))


def begins(sizes):
    return [sum(sizes[:i]) for i in range(len(sizes))]


def step_of(factor, values, v):
    return sum(factor[i] * (value[...] - v) for i, value in enumerate(values))


def step_chunks(factor, values, v, start, sizes):
    columns, tile, count = v.shape[1], UNIT, len(values)
    places = begins(sizes)

    def kernel(factor, *refs):
        values, v, outs = refs[:count], refs[count], refs[count + 1 :]
        i = pl.program_id(0)
        total = step_of(factor, values, v[...])
        for out, begin, size in zip(outs, places, sizes):

            @pl.when((i >= begin) & (i < begin + size))
            def _(out=out):
                out[...] = total

    at = pl.BlockSpec((tile, columns), lambda i: (start + i, 0))
    outs = [group_spec(begin, size, tile, columns) for begin, size in zip(places, sizes)]
    shapes = [jax.ShapeDtypeStruct((size * tile, columns), v.dtype) for size in sizes]
    moved = (count + 2) * sum(sizes) * tile * columns
    in_specs = [SMEM] + [at] * (count + 1)
    return run(kernel, (sum(sizes),), in_specs, outs, shapes, (factor, *values, v), moved)


def move_chunks(is_end, share, totals, backs, values, v, start, sizes, carried):
    columns, tile, count, chunks = v.shape[1], UNIT, len(values), len(sizes)
    places = begins(sizes)

    def kernel(is_end, v, *refs):
        values, rest = refs[:count], refs[count:]
        totals, backs, (v_out, sq_out) = rest[:chunks], rest[chunks : 2 * chunks], rest[-2:]
        i = pl.program_id(0)

        @pl.when(i == 0)
        def _():
            sq_out[...] = rest[-3][...] if carried else jnp.zeros_like(sq_out)

        for total, back, begin, size in zip(totals, backs, places, sizes):

            @pl.when((i >= begin) & (i < begin + size))
            def _(total=total, back=back):
                step = jnp.where(is_end[0] > 0, back[...], total[...])
                v_out[...] = v[...] + step * share

        moved = v_out[...]
        for k, value in enumerate(values):
            square = jnp.square(value[...] - moved)
            folded = sum(square[j : j + 8] for j in range(0, tile, 8))
            sq_out[k] += sum(folded[:, j : j + 128] for j in range(0, columns, 128))

    at = pl.BlockSpec((tile, columns), lambda i, _: (start + i, 0))
    squares = pl.BlockSpec((count, 8, 128), lambda i, _: (0, 0, 0))

    def part(begin, size, wanted):
        def index(i, is_end):
            return (jnp.where(is_end[0] == wanted, jnp.clip(i - begin, 0, size - 1), 0), 0)

        return pl.BlockSpec((tile, columns), index)

    parts = [part(*place, wanted) for wanted in (0, 1) for place in zip(places, sizes)]
    in_specs = [at] * (count + 1) + parts
    operands = (is_end, v, *values, *totals, *backs)
    aliases = {}
    if carried:
        in_specs += [pl.BlockSpec(memory_space=pl.ANY), squares]
        aliases = {len(operands): 0, len(operands) + 1: 1}
        operands += tuple(carried)
    shapes = (
        jax.ShapeDtypeStruct(v.shape, v.dtype),
        jax.ShapeDtypeStruct((count, 8, 128), v.dtype),
    )
    moved = (count + 4) * sum(sizes) * tile * columns
    return run(kernel, (sum(sizes),), in_specs, (at, squares), shapes, operands, moved, aliases, prefetch=1)


def step_blocks(places, factor, values, v):
    _, rest, columns = v.shape
    count, blocks, parts = len(values), len(places), 4
    width = columns // parts

    def kernel(places, factor, *refs):
        values, v, outs = refs[:count], refs[count], refs[count + 1 :]
        total = step_of(factor, values, v[...])
        for k, out in enumerate(outs):

            @pl.when(pl.program_id(0) == k)
            def _(out=out):
                out[...] = total

    at = pl.BlockSpec((None, rest, width), lambda b, i, places: (places[b], 0, i))
    outs = [
        pl.BlockSpec(
            (rest, width), lambda b, i, _, k=k: (0, jnp.clip((b - k) * parts + i, 0, parts - 1))
        )
        for k in range(blocks)
    ]
    shapes = [jax.ShapeDtypeStruct((rest, columns), v.dtype)] * blocks
    moved = (count + 2) * blocks * rest * columns
    operands = (jnp.stack(places).astype(jnp.int32), factor, *values, v)
    in_specs = [SMEM] + [at] * (count + 1)
    return run(kernel, (blocks, parts), in_specs, outs, shapes, operands, moved, prefetch=1)


def move_spread(share, factor, values, v):
    (rows, columns), count = v.shape, values.shape[0]
    tile = 2 * TILE if rows % (2 * TILE) == 0 else TILE

    def kernel(factor, v, values, v_out, sq_out):
        base = v[...]
        moved = base + sum(factor[k] * (values[k] - base) for k in range(count)) * share
        v_out[...] = moved

        @pl.when(pl.program_id(0) == 0)
        def _():
            sq_out[...] = jnp.zeros_like(sq_out)

        for k in range(count):
            square = jnp.square(values[k] - moved)
            folded = sum(square[j : j + TILE] for j in range(0, tile, TILE))
            sq_out[k] += sum(folded[:, j : j + 128] for j in range(0, columns, 128))

    at = pl.BlockSpec((tile, columns), lambda i: (i, 0))
    stack = pl.BlockSpec((count, tile, columns), lambda i: (0, i, 0))
    squares = pl.BlockSpec((count, TILE, 128), lambda i: (0, 0, 0))
    shapes = (
        jax.ShapeDtypeStruct(v.shape, v.dtype),
        jax.ShapeDtypeStruct((count, TILE, 128), v.dtype),
    )
    moved = (count + 2) * rows * columns
    operands = (factor, v, values)
    return run(kernel, (rows // tile,), [SMEM, at, stack], (at, squares), shapes, operands, moved)


def spread_only(mine, center, radius_total, worker_count):
    own_rows = center
    gathered = lax.all_to_all(mine, ("worker", "outer"), split_axis=0, concat_axis=0, tiled=True)
    for _ in range(ITERS):
        difference = gathered - own_rows[None]
        norm_sq = sum_over_devices(jnp.sum(difference * difference, axis=(1, 2)))
        factor = jnp.minimum(1.0, radius_total * lax.rsqrt(norm_sq + epsilon))
        own_rows = own_rows + jnp.sum(factor[:, None, None] * difference, axis=0) / worker_count
    return own_rows


def on_device(grads, center, radius):
    workers, outers = lax.axis_size("worker"), lax.axis_size("outer")
    worker_count = workers * outers
    radius_total = radius[0] * math.sqrt(D * KVW)
    rows, columns = center.shape
    mine = grads.reshape(worker_count, rows, columns)
    plan = split(rows, outers)
    if plan is None:
        return spread_only(mine, center, radius_total, worker_count)
    cut, sizes = plan
    rest = rows - cut

    w, o = lax.axis_index("worker"), lax.axis_index("outer")
    is_end = (o == 0) | (o == LINE - 1)
    is_low = o < LINE // 2

    def line_rows(source, worker):
        return lax.dynamic_slice(source, (worker * outers, cut, 0), (outers, rest, columns))

    tail = center[cut:]
    pair = send(tail, [(i, i ^ 1) for i in range(LINE)])
    steps = list(range(workers // 2, workers)) + list(range(1, workers // 2)) + [0]
    held, source = [], mine
    for step in steps:
        sent = line_rows(source, w ^ step)
        source = tie(source, sent)
        if step:
            swap = [(i, i ^ step) for i in range(workers)]
            sent = send(sent, swap, "worker")
        held.append(sent)
    spread = lax.all_to_all(
        mine[:, :cut], ("worker", "outer"), split_axis=0, concat_axis=0, tiled=True
    )
    first = (o % 2) == 0
    near = [jnp.where(first, tail, pair), jnp.where(first, pair, tail)]
    far = []
    for part in (tail, pair):
        crossed = send(part, ACROSS)
        far.append(jnp.where(is_end, send(crossed, TO_ENDS), crossed))
    low, high = near + far, far[::-1] + near
    line_v = jnp.stack([jnp.where(is_low, *parts) for parts in zip(low, high)])
    spread_v, share = center[:cut], 1 / worker_count

    places = jnp.stack([(w ^ step) * outers + o for step in steps])
    hit = places[:, None] == jnp.arange(worker_count)[None]

    def placed(line_sq):
        return jnp.sum(jnp.where(hit, line_sq[:, None], 0.0), axis=0)

    def factors(both):
        norm_sq = sum_over_devices(both)
        factor = jnp.minimum(1.0, radius_total * lax.rsqrt(norm_sq + epsilon))
        return factor, jnp.sum(jnp.where(hit, factor[None], 0.0), axis=1)

    line_sq, v = jnp.zeros((worker_count,), jnp.float32), line_v
    for place in reversed(range(workers)):
        square = jnp.sum(jnp.square(held[place] - v))
        line_sq = lax.optimization_barrier(line_sq + jnp.where(hit[place], square, 0.0))
        v = tie(v, line_sq)
    spread_sq = jnp.sum(jnp.square(spread - spread_v[None]), axis=(1, 2))
    factor, line_factor = factors(spread_sq + line_sq)

    flat = [value.reshape(outers * rest, columns) for value in held]
    flat_v = line_v.reshape(outers * rest, columns)
    end_flag = is_end.astype(jnp.int32).reshape(1)
    next_spread_v, spread_sq = move_spread(share, factor, spread, spread_v)
    early = {3: next_spread_v}
    count, places = len(sizes), begins(sizes)
    own = step_chunks(line_factor, flat, flat_v, 0, sizes[:1])
    own += step_chunks(line_factor, flat, tie(flat_v, own[0]), places[1], sizes[1:2])
    own += step_chunks(line_factor, flat, tie(flat_v, own[1]), places[2], sizes[2:4])
    own += step_chunks(line_factor, flat, tie(flat_v, own[2]), places[4], sizes[4:])
    cuts = [0, count - 4, count - 2, count]
    groups = [slice(*pair) for pair in zip(cuts, cuts[1:])]
    totals, backs, carried = [], [], ()

    def move(part, carried):
        return move_chunks(
            end_flag, share, totals[part], backs[part], flat, flat_v,
            places[part.start], sizes[part], carried,
        )

    for chunk in range(count):
        got = send(own[chunk], TO_MIDS)
        if chunk >= 2:
            got = tie(got, totals[chunk - 2])
        total = own[chunk] + got
        total = total + send(total, ACROSS)
        if chunk in early:
            total = tie(total, early[chunk])
        totals.append(total)
        backs.append(send(total, TO_ENDS))
    carried = move(groups[0], carried)
    for part in groups[1:]:
        carried = move(part, carried)
    spread_v = next_spread_v
    flat_v = carried[0]
    line_v = flat_v.reshape(line_v.shape)
    spread_sq = lax.optimization_barrier(jnp.sum(spread_sq, axis=(1, 2)))
    factor, line_factor = factors(spread_sq + placed(jnp.sum(carried[1], axis=(1, 2))))

    order = [jnp.where(is_low, LINE - 1 - place, place) for place in range(LINE)]
    block = step_blocks(order[:1], line_factor, held, line_v)
    block += step_blocks(order[1:], line_factor, held, tie(line_v, block[0]))
    arrived = [send(block[place], TO_MIDS) for place in range(3)]
    passed = [send(block[place] + arrived[place], ACROSS) for place in range(2)]
    last = send(block[3] + passed[0], TO_ENDS)
    own_v = lax.dynamic_index_in_dim(line_v, o, 0, keepdims=False)
    own_v = lax.optimization_barrier(own_v + jnp.where(is_end, block[3], block[2]) * share)
    own_v = own_v + jnp.where(is_end, last, arrived[2] + passed[1]) * share
    step = jnp.sum(factor[:, None, None] * (spread - spread_v[None]), axis=0)
    buffer = lax.optimization_barrier(jnp.pad(spread_v + step * share, ((0, rest), (0, 0))))
    return lax.dynamic_update_slice(buffer, own_v, (cut, 0))


def solution(mesh):
    in_specs = (P("worker", "outer", None, "mp"), P(("worker", "outer"), "mp"), P())
    out_specs = P(("worker", "outer"), "mp")

    return jax.shard_map(on_device, mesh=mesh, in_specs=in_specs, out_specs=out_specs, check_vma=False)
```

```python
import math

import jax
import jax.numpy as jnp
from jax import lax
from jax.experimental import pallas as pl
from jax.experimental.pallas import tpu as pltpu
from jax.sharding import PartitionSpec as P


D = 3584
ITERS = 2
KVW = 4096
AXES = ("worker", "outer", "mp")
LINE = 4
TILE = 8
UNIT = 16
SPREAD = 3 / 7

GRANT = 60 << 20
SMALL_GRANT = 8 << 20

epsilon = 1e-06


def sum_over_devices(value):
    for axis in AXES:
        size = lax.axis_size(axis)
        step = 1
        while step < size:
            value = value + lax.ppermute(value, axis, [(i, i ^ step) for i in range(size)])
            step *= 2
    return value


def send(value, pairs, axis="outer"):
    return lax.ppermute(value, axis, pairs)


TO_MIDS = [(0, 1), (3, 2)]
ACROSS = [(1, 2), (2, 1)]
TO_ENDS = [(1, 0), (2, 3)]


def tie(value, earlier):
    return lax.optimization_barrier((value, earlier))[0]


def split(rows, outers):
    cut = int(rows * SPREAD) // TILE * TILE
    rest = rows - cut
    units = rest * outers // UNIT
    if outers != LINE or rest % TILE or units < 22 or not cut:
        return None
    body = units - 4
    sizes = [2] + [4] * (body // 4) + [body % 4] * (body % 4 > 0) + [2]
    return cut, sizes


SMEM = pl.BlockSpec(memory_space=pltpu.SMEM)


def run(
    kernel, grid, in_specs, out_specs, out_shape, operands, moved, aliases={}, prefetch=0, grant=GRANT
):
    return pl.pallas_call(
        kernel,
        grid_spec=pltpu.PrefetchScalarGridSpec(
            num_scalar_prefetch=prefetch, grid=grid, in_specs=in_specs, out_specs=out_specs
        ),
        out_shape=out_shape,
        input_output_aliases=aliases,
        compiler_params=pltpu.CompilerParams(vmem_limit_bytes=grant),
        cost_estimate=pl.CostEstimate(flops=4 * moved, bytes_accessed=4 * moved, transcendentals=0),
    )(*operands)


def group_spec(begin, count, tile, columns):
    return pl.BlockSpec((tile, columns), lambda i: (jnp.clip(i - begin, 0, count - 1), 0))


def begins(sizes):
    return [sum(sizes[:i]) for i in range(len(sizes))]


def step_of(factor, values, v):
    return sum(factor[i] * (value[...] - v) for i, value in enumerate(values))


def step_chunks(factor, values, v, start, sizes):
    columns, tile, count = v.shape[1], UNIT, len(values)
    places = begins(sizes)

    def kernel(factor, *refs):
        values, v, outs = refs[:count], refs[count], refs[count + 1 :]
        i = pl.program_id(0)
        total = step_of(factor, values, v[...])
        for out, begin, size in zip(outs, places, sizes):

            @pl.when((i >= begin) & (i < begin + size))
            def _(out=out):
                out[...] = total

    at = pl.BlockSpec((tile, columns), lambda i: (start + i, 0))
    outs = [group_spec(begin, size, tile, columns) for begin, size in zip(places, sizes)]
    shapes = [jax.ShapeDtypeStruct((size * tile, columns), v.dtype) for size in sizes]
    moved = (count + 2) * sum(sizes) * tile * columns
    in_specs = [SMEM] + [at] * (count + 1)
    return run(kernel, (sum(sizes),), in_specs, outs, shapes, (factor, *values, v), moved, grant=SMALL_GRANT)


def move_chunks(is_end, share, totals, backs, values, v, start, sizes, carried):
    columns, tile, count, chunks = v.shape[1], UNIT, len(values), len(sizes)
    places = begins(sizes)

    def kernel(is_end, v, *refs):
        values, rest = refs[:count], refs[count:]
        totals, backs, (v_out, sq_out) = rest[:chunks], rest[chunks : 2 * chunks], rest[-2:]
        i = pl.program_id(0)

        @pl.when(i == 0)
        def _():
            sq_out[...] = rest[-3][...] if carried else jnp.zeros_like(sq_out)

        for total, back, begin, size in zip(totals, backs, places, sizes):

            @pl.when((i >= begin) & (i < begin + size))
            def _(total=total, back=back):
                step = jnp.where(is_end[0] > 0, back[...], total[...])
                v_out[...] = v[...] + step * share

        moved = v_out[...]
        for k, value in enumerate(values):
            square = jnp.square(value[...] - moved)
            folded = sum(square[j : j + 8] for j in range(0, tile, 8))
            sq_out[k] += sum(folded[:, j : j + 128] for j in range(0, columns, 128))

    at = pl.BlockSpec((tile, columns), lambda i, _: (start + i, 0))
    squares = pl.BlockSpec((count, 8, 128), lambda i, _: (0, 0, 0))

    def part(begin, size, wanted):
        def index(i, is_end):
            return (jnp.where(is_end[0] == wanted, jnp.clip(i - begin, 0, size - 1), 0), 0)

        return pl.BlockSpec((tile, columns), index)

    parts = [part(*place, wanted) for wanted in (0, 1) for place in zip(places, sizes)]
    in_specs = [at] * (count + 1) + parts
    operands = (is_end, v, *values, *totals, *backs)
    aliases = {}
    if carried:
        in_specs += [pl.BlockSpec(memory_space=pl.ANY), squares]
        aliases = {len(operands): 0, len(operands) + 1: 1}
        operands += tuple(carried)
    shapes = (
        jax.ShapeDtypeStruct(v.shape, v.dtype),
        jax.ShapeDtypeStruct((count, 8, 128), v.dtype),
    )
    moved = (count + 4) * sum(sizes) * tile * columns
    return run(kernel, (sum(sizes),), in_specs, (at, squares), shapes, operands, moved, aliases, prefetch=1)


def step_blocks(places, factor, values, v):
    _, rest, columns = v.shape
    count, blocks, parts = len(values), len(places), 4
    width = columns // parts

    def kernel(places, factor, *refs):
        values, v, outs = refs[:count], refs[count], refs[count + 1 :]
        total = step_of(factor, values, v[...])
        for k, out in enumerate(outs):

            @pl.when(pl.program_id(0) == k)
            def _(out=out):
                out[...] = total

    at = pl.BlockSpec((None, rest, width), lambda b, i, places: (places[b], 0, i))
    outs = [
        pl.BlockSpec(
            (rest, width), lambda b, i, _, k=k: (0, jnp.clip((b - k) * parts + i, 0, parts - 1))
        )
        for k in range(blocks)
    ]
    shapes = [jax.ShapeDtypeStruct((rest, columns), v.dtype)] * blocks
    moved = (count + 2) * blocks * rest * columns
    operands = (jnp.stack(places).astype(jnp.int32), factor, *values, v)
    in_specs = [SMEM] + [at] * (count + 1)
    return run(kernel, (blocks, parts), in_specs, outs, shapes, operands, moved, prefetch=1)


def move_spread(share, factor, values, v):
    (rows, columns), count = v.shape, values.shape[0]
    tile = 2 * TILE if rows % (2 * TILE) == 0 else TILE

    def kernel(factor, v, values, v_out, sq_out):
        base = v[...]
        moved = base + sum(factor[k] * (values[k] - base) for k in range(count)) * share
        v_out[...] = moved

        @pl.when(pl.program_id(0) == 0)
        def _():
            sq_out[...] = jnp.zeros_like(sq_out)

        for k in range(count):
            square = jnp.square(values[k] - moved)
            folded = sum(square[j : j + TILE] for j in range(0, tile, TILE))
            sq_out[k] += sum(folded[:, j : j + 128] for j in range(0, columns, 128))

    at = pl.BlockSpec((tile, columns), lambda i: (i, 0))
    stack = pl.BlockSpec((count, tile, columns), lambda i: (0, i, 0))
    squares = pl.BlockSpec((count, TILE, 128), lambda i: (0, 0, 0))
    shapes = (
        jax.ShapeDtypeStruct(v.shape, v.dtype),
        jax.ShapeDtypeStruct((count, TILE, 128), v.dtype),
    )
    moved = (count + 2) * rows * columns
    operands = (factor, v, values)
    specs = [SMEM, at, stack], (at, squares)
    return run(kernel, (rows // tile,), *specs, shapes, operands, moved, grant=SMALL_GRANT + (8 << 20))


def spread_only(mine, center, radius_total, worker_count):
    own_rows = center
    gathered = lax.all_to_all(mine, ("worker", "outer"), split_axis=0, concat_axis=0, tiled=True)
    for _ in range(ITERS):
        difference = gathered - own_rows[None]
        norm_sq = sum_over_devices(jnp.sum(difference * difference, axis=(1, 2)))
        factor = jnp.minimum(1.0, radius_total * lax.rsqrt(norm_sq + epsilon))
        own_rows = own_rows + jnp.sum(factor[:, None, None] * difference, axis=0) / worker_count
    return own_rows


def on_device(grads, center, radius):
    workers, outers = lax.axis_size("worker"), lax.axis_size("outer")
    worker_count = workers * outers
    radius_total = radius[0] * math.sqrt(D * KVW)
    rows, columns = center.shape
    mine = grads.reshape(worker_count, rows, columns)
    plan = split(rows, outers)
    if plan is None:
        return spread_only(mine, center, radius_total, worker_count)
    cut, sizes = plan
    rest = rows - cut

    w, o = lax.axis_index("worker"), lax.axis_index("outer")
    is_end = (o == 0) | (o == LINE - 1)
    is_low = o < LINE // 2

    def line_rows(source, worker):
        return lax.dynamic_slice(source, (worker * outers, cut, 0), (outers, rest, columns))

    tail = center[cut:]
    pair = send(tail, [(i, i ^ 1) for i in range(LINE)])
    steps = list(range(workers // 2, workers)) + list(range(1, workers // 2)) + [0]
    held, source = [], mine
    for step in steps:
        sent = line_rows(source, w ^ step)
        source = tie(source, sent)
        if step:
            swap = [(i, i ^ step) for i in range(workers)]
            sent = send(sent, swap, "worker")
        held.append(sent)
    spread = lax.all_to_all(
        mine[:, :cut], ("worker", "outer"), split_axis=0, concat_axis=0, tiled=True
    )
    first = (o % 2) == 0
    near = [jnp.where(first, tail, pair), jnp.where(first, pair, tail)]
    far = []
    for part in (tail, pair):
        crossed = send(part, ACROSS)
        far.append(jnp.where(is_end, send(crossed, TO_ENDS), crossed))
    low, high = near + far, far[::-1] + near
    line_v = jnp.stack([jnp.where(is_low, *parts) for parts in zip(low, high)])
    spread_v, share = center[:cut], 1 / worker_count

    places = jnp.stack([(w ^ step) * outers + o for step in steps])
    hit = places[:, None] == jnp.arange(worker_count)[None]

    def placed(line_sq):
        return jnp.sum(jnp.where(hit, line_sq[:, None], 0.0), axis=0)

    def factors(both):
        norm_sq = sum_over_devices(both)
        factor = jnp.minimum(1.0, radius_total * lax.rsqrt(norm_sq + epsilon))
        return factor, jnp.sum(jnp.where(hit, factor[None], 0.0), axis=1)

    line_sq, v = jnp.zeros((worker_count,), jnp.float32), line_v
    for place in reversed(range(workers)):
        square = jnp.sum(jnp.square(held[place] - v))
        line_sq = lax.optimization_barrier(line_sq + jnp.where(hit[place], square, 0.0))
        v = tie(v, line_sq)
    spread_sq = jnp.sum(jnp.square(spread - spread_v[None]), axis=(1, 2))
    factor, line_factor = factors(spread_sq + line_sq)

    flat = [value.reshape(outers * rest, columns) for value in held]
    flat_v = line_v.reshape(outers * rest, columns)
    end_flag = is_end.astype(jnp.int32).reshape(1)
    next_spread_v, spread_sq = move_spread(share, factor, spread, spread_v)
    early = {2: next_spread_v}
    count, places = len(sizes), begins(sizes)
    own = step_chunks(line_factor, flat, flat_v, 0, sizes[:1])
    own += step_chunks(line_factor, flat, tie(flat_v, own[0]), places[1], sizes[1:2])
    own += step_chunks(line_factor, flat, tie(flat_v, own[1]), places[2], sizes[2:4])
    own += step_chunks(line_factor, flat, tie(flat_v, own[2]), places[4], sizes[4:])
    cuts = [0, count - 5, count - 3, count - 2, count - 1, count]
    groups = [slice(*pair) for pair in zip(cuts, cuts[1:])]
    totals, backs, carried = [], [], ()

    def move(part, carried):
        return move_chunks(
            end_flag, share, totals[part], backs[part], flat, flat_v,
            places[part.start], sizes[part], carried,
        )

    for chunk in range(count):
        got = send(own[chunk], TO_MIDS)
        if chunk >= 2:
            got = tie(got, totals[chunk - 2])
        total = own[chunk] + got
        total = total + send(total, ACROSS)
        if chunk in early:
            total = tie(total, early[chunk])
        if chunk == count - 3:
            carried = move(groups[0], carried)
            total = tie(total, carried[1])
        totals.append(total)
        backs.append(send(total, TO_ENDS))
    carried = move(groups[1], carried)
    for part in groups[2:]:
        carried = move(part, carried)
    spread_v = next_spread_v
    flat_v = carried[0]
    line_v = flat_v.reshape(line_v.shape)
    spread_sq = lax.optimization_barrier(jnp.sum(spread_sq, axis=(1, 2)))
    factor, line_factor = factors(spread_sq + placed(jnp.sum(carried[1], axis=(1, 2))))

    order = [jnp.where(is_low, LINE - 1 - place, place) for place in range(LINE)]
    block = step_blocks(order[:1], line_factor, held, line_v)
    block += step_blocks(order[1:], line_factor, held, tie(line_v, block[0]))
    arrived = [send(block[place], TO_MIDS) for place in range(3)]
    passed = [send(block[place] + arrived[place], ACROSS) for place in range(2)]
    last = send(block[3] + passed[0], TO_ENDS)
    own_v = lax.dynamic_index_in_dim(line_v, o, 0, keepdims=False)
    own_v = lax.optimization_barrier(own_v + jnp.where(is_end, block[3], block[2]) * share)
    own_v = own_v + jnp.where(is_end, last, arrived[2] + passed[1]) * share
    step = jnp.sum(factor[:, None, None] * (spread - spread_v[None]), axis=0)
    buffer = lax.optimization_barrier(jnp.pad(spread_v + step * share, ((0, rest), (0, 0))))
    return lax.dynamic_update_slice(buffer, own_v, (cut, 0))


def solution(mesh):
    in_specs = (P("worker", "outer", None, "mp"), P(("worker", "outer"), "mp"), P())
    out_specs = P(("worker", "outer"), "mp")

    return jax.shard_map(on_device, mesh=mesh, in_specs=in_specs, out_specs=out_specs, check_vma=False)
```

```python
import math

import jax
import jax.numpy as jnp
from jax import lax
from jax.experimental import pallas as pl
from jax.experimental.pallas import tpu as pltpu
from jax.sharding import PartitionSpec as P


D = 3584
ITERS = 2
KVW = 4096
AXES = ("worker", "outer", "mp")
LINE = 4
TILE = 8
UNIT = 16
SPREAD = 3 / 7

GRANT = 60 << 20
SMALL_GRANT = 8 << 20

epsilon = 1e-06


def sum_over_devices(value):
    for axis in AXES:
        size = lax.axis_size(axis)
        step = 1
        while step < size:
            value = value + lax.ppermute(value, axis, [(i, i ^ step) for i in range(size)])
            step *= 2
    return value


def send(value, pairs, axis="outer"):
    return lax.ppermute(value, axis, pairs)


TO_MIDS = [(0, 1), (3, 2)]
ACROSS = [(1, 2), (2, 1)]
TO_ENDS = [(1, 0), (2, 3)]


def tie(value, earlier):
    return lax.optimization_barrier((value, earlier))[0]


def split(rows, outers):
    cut = int(rows * SPREAD) // TILE * TILE
    rest = rows - cut
    units = rest * outers // UNIT
    if outers != LINE or rest % TILE or units < 22 or not cut:
        return None
    body = units - 12
    sizes = [2, 4] + [5] * (body // 5) + [body % 5] * (body % 5 > 0) + [4, 2]
    return cut, sizes


SMEM = pl.BlockSpec(memory_space=pltpu.SMEM)


def run(
    kernel, grid, in_specs, out_specs, out_shape, operands, moved, aliases={}, prefetch=0, grant=GRANT
):
    return pl.pallas_call(
        kernel,
        grid_spec=pltpu.PrefetchScalarGridSpec(
            num_scalar_prefetch=prefetch, grid=grid, in_specs=in_specs, out_specs=out_specs
        ),
        out_shape=out_shape,
        input_output_aliases=aliases,
        compiler_params=pltpu.CompilerParams(vmem_limit_bytes=grant),
        cost_estimate=pl.CostEstimate(flops=4 * moved, bytes_accessed=4 * moved, transcendentals=0),
    )(*operands)


def group_spec(begin, count, tile, columns):
    return pl.BlockSpec((tile, columns), lambda i: (jnp.clip(i - begin, 0, count - 1), 0))


def begins(sizes):
    return [sum(sizes[:i]) for i in range(len(sizes))]


def step_of(factor, values, v):
    return sum(factor[i] * (value[...] - v) for i, value in enumerate(values))


def step_chunks(factor, values, v, start, sizes):
    columns, tile, count = v.shape[1], UNIT, len(values)
    places = begins(sizes)

    def kernel(factor, *refs):
        values, v, outs = refs[:count], refs[count], refs[count + 1 :]
        i = pl.program_id(0)
        total = step_of(factor, values, v[...])
        for out, begin, size in zip(outs, places, sizes):

            @pl.when((i >= begin) & (i < begin + size))
            def _(out=out):
                out[...] = total

    at = pl.BlockSpec((tile, columns), lambda i: (start + i, 0))
    outs = [group_spec(begin, size, tile, columns) for begin, size in zip(places, sizes)]
    shapes = [jax.ShapeDtypeStruct((size * tile, columns), v.dtype) for size in sizes]
    moved = (count + 2) * sum(sizes) * tile * columns
    in_specs = [SMEM] + [at] * (count + 1)
    return run(kernel, (sum(sizes),), in_specs, outs, shapes, (factor, *values, v), moved, grant=SMALL_GRANT)


def move_chunks(is_end, share, totals, backs, values, v, start, sizes, carried):
    columns, tile, count, chunks = v.shape[1], UNIT, len(values), len(sizes)
    places = begins(sizes)

    def kernel(is_end, v, *refs):
        values, rest = refs[:count], refs[count:]
        totals, backs, (v_out, sq_out) = rest[:chunks], rest[chunks : 2 * chunks], rest[-2:]
        i = pl.program_id(0)

        @pl.when(i == 0)
        def _():
            sq_out[...] = rest[-3][...] if carried else jnp.zeros_like(sq_out)

        for total, back, begin, size in zip(totals, backs, places, sizes):

            @pl.when((i >= begin) & (i < begin + size))
            def _(total=total, back=back):
                step = jnp.where(is_end[0] > 0, back[...], total[...])
                v_out[...] = v[...] + step * share

        moved = v_out[...]
        for k, value in enumerate(values):
            square = jnp.square(value[...] - moved)
            folded = sum(square[j : j + 8] for j in range(0, tile, 8))
            sq_out[k] += sum(folded[:, j : j + 128] for j in range(0, columns, 128))

    at = pl.BlockSpec((tile, columns), lambda i, _: (start + i, 0))
    squares = pl.BlockSpec((count, 8, 128), lambda i, _: (0, 0, 0))

    def part(begin, size, wanted):
        def index(i, is_end):
            return (jnp.where(is_end[0] == wanted, jnp.clip(i - begin, 0, size - 1), 0), 0)

        return pl.BlockSpec((tile, columns), index)

    parts = [part(*place, wanted) for wanted in (0, 1) for place in zip(places, sizes)]
    in_specs = [at] * (count + 1) + parts
    operands = (is_end, v, *values, *totals, *backs)
    aliases = {}
    if carried:
        in_specs += [pl.BlockSpec(memory_space=pl.ANY), squares]
        aliases = {len(operands): 0, len(operands) + 1: 1}
        operands += tuple(carried)
    shapes = (
        jax.ShapeDtypeStruct(v.shape, v.dtype),
        jax.ShapeDtypeStruct((count, 8, 128), v.dtype),
    )
    moved = (count + 4) * sum(sizes) * tile * columns
    return run(kernel, (sum(sizes),), in_specs, (at, squares), shapes, operands, moved, aliases, prefetch=1)


def step_blocks(places, factor, values, v):
    _, rest, columns = v.shape
    count, blocks, parts = len(values), len(places), 4
    width = columns // parts

    def kernel(places, factor, *refs):
        values, v, outs = refs[:count], refs[count], refs[count + 1 :]
        total = step_of(factor, values, v[...])
        for k, out in enumerate(outs):

            @pl.when(pl.program_id(0) == k)
            def _(out=out):
                out[...] = total

    at = pl.BlockSpec((None, rest, width), lambda b, i, places: (places[b], 0, i))
    outs = [
        pl.BlockSpec(
            (rest, width), lambda b, i, _, k=k: (0, jnp.clip((b - k) * parts + i, 0, parts - 1))
        )
        for k in range(blocks)
    ]
    shapes = [jax.ShapeDtypeStruct((rest, columns), v.dtype)] * blocks
    moved = (count + 2) * blocks * rest * columns
    operands = (jnp.stack(places).astype(jnp.int32), factor, *values, v)
    in_specs = [SMEM] + [at] * (count + 1)
    return run(kernel, (blocks, parts), in_specs, outs, shapes, operands, moved, prefetch=1)


def move_spread(share, factor, values, v):
    (rows, columns), count = v.shape, values.shape[0]
    tile = 2 * TILE if rows % (2 * TILE) == 0 else TILE

    def kernel(factor, v, values, v_out, sq_out):
        base = v[...]
        moved = base + sum(factor[k] * (values[k] - base) for k in range(count)) * share
        v_out[...] = moved

        @pl.when(pl.program_id(0) == 0)
        def _():
            sq_out[...] = jnp.zeros_like(sq_out)

        for k in range(count):
            square = jnp.square(values[k] - moved)
            folded = sum(square[j : j + TILE] for j in range(0, tile, TILE))
            sq_out[k] += sum(folded[:, j : j + 128] for j in range(0, columns, 128))

    at = pl.BlockSpec((tile, columns), lambda i: (i, 0))
    stack = pl.BlockSpec((count, tile, columns), lambda i: (0, i, 0))
    squares = pl.BlockSpec((count, TILE, 128), lambda i: (0, 0, 0))
    shapes = (
        jax.ShapeDtypeStruct(v.shape, v.dtype),
        jax.ShapeDtypeStruct((count, TILE, 128), v.dtype),
    )
    moved = (count + 2) * rows * columns
    operands = (factor, v, values)
    specs = [SMEM, at, stack], (at, squares)
    return run(kernel, (rows // tile,), *specs, shapes, operands, moved, grant=SMALL_GRANT + (8 << 20))


def spread_only(mine, center, radius_total, worker_count):
    own_rows = center
    gathered = lax.all_to_all(mine, ("worker", "outer"), split_axis=0, concat_axis=0, tiled=True)
    for _ in range(ITERS):
        difference = gathered - own_rows[None]
        norm_sq = sum_over_devices(jnp.sum(difference * difference, axis=(1, 2)))
        factor = jnp.minimum(1.0, radius_total * lax.rsqrt(norm_sq + epsilon))
        own_rows = own_rows + jnp.sum(factor[:, None, None] * difference, axis=0) / worker_count
    return own_rows


def on_device(grads, center, radius):
    workers, outers = lax.axis_size("worker"), lax.axis_size("outer")
    worker_count = workers * outers
    radius_total = radius[0] * math.sqrt(D * KVW)
    rows, columns = center.shape
    mine = grads.reshape(worker_count, rows, columns)
    plan = split(rows, outers)
    if plan is None:
        return spread_only(mine, center, radius_total, worker_count)
    cut, sizes = plan
    rest = rows - cut

    w, o = lax.axis_index("worker"), lax.axis_index("outer")
    is_end = (o == 0) | (o == LINE - 1)
    is_low = o < LINE // 2

    def line_rows(source, worker):
        return lax.dynamic_slice(source, (worker * outers, cut, 0), (outers, rest, columns))

    tail = center[cut:]
    pair = send(tail, [(i, i ^ 1) for i in range(LINE)])
    steps = list(range(workers // 2, workers)) + list(range(1, workers // 2)) + [0]
    held, source = [], mine
    for step in steps:
        sent = line_rows(source, w ^ step)
        source = tie(source, sent)
        if step:
            swap = [(i, i ^ step) for i in range(workers)]
            sent = send(sent, swap, "worker")
        held.append(sent)
    spread = lax.all_to_all(
        mine[:, :cut], ("worker", "outer"), split_axis=0, concat_axis=0, tiled=True
    )
    first = (o % 2) == 0
    near = [jnp.where(first, tail, pair), jnp.where(first, pair, tail)]
    far = []
    for part in (tail, pair):
        crossed = send(part, ACROSS)
        far.append(jnp.where(is_end, send(crossed, TO_ENDS), crossed))
    low, high = near + far, far[::-1] + near
    line_v = jnp.stack([jnp.where(is_low, *parts) for parts in zip(low, high)])
    spread_v, share = center[:cut], 1 / worker_count

    places = jnp.stack([(w ^ step) * outers + o for step in steps])
    hit = places[:, None] == jnp.arange(worker_count)[None]

    def placed(line_sq):
        return jnp.sum(jnp.where(hit, line_sq[:, None], 0.0), axis=0)

    def factors(both):
        norm_sq = sum_over_devices(both)
        factor = jnp.minimum(1.0, radius_total * lax.rsqrt(norm_sq + epsilon))
        return factor, jnp.sum(jnp.where(hit, factor[None], 0.0), axis=1)

    line_sq, v = jnp.zeros((worker_count,), jnp.float32), line_v
    for place in [workers - 1, *range(workers // 2, workers - 1), *range(workers // 2)]:
        square = jnp.sum(jnp.square(held[place] - v))
        line_sq = lax.optimization_barrier(line_sq + jnp.where(hit[place], square, 0.0))
        v = tie(v, line_sq)
    spread_sq = jnp.sum(jnp.square(spread - spread_v[None]), axis=(1, 2))
    factor, line_factor = factors(spread_sq + line_sq)

    flat = [value.reshape(outers * rest, columns) for value in held]
    flat_v = line_v.reshape(outers * rest, columns)
    end_flag = is_end.astype(jnp.int32).reshape(1)
    next_spread_v, spread_sq = move_spread(share, factor, spread, spread_v)
    early = {3: next_spread_v}
    count, places = len(sizes), begins(sizes)
    own = step_chunks(line_factor, flat, flat_v, 0, sizes[:1])
    own += step_chunks(line_factor, flat, tie(flat_v, own[0]), places[1], sizes[1:2])
    own += step_chunks(line_factor, flat, tie(flat_v, own[1]), places[2], sizes[2:4])
    own += step_chunks(line_factor, flat, tie(flat_v, own[2]), places[4], sizes[4:])
    cuts = [0, count - 5, count - 3, count - 2, count - 1, count]
    groups = [slice(*pair) for pair in zip(cuts, cuts[1:])]
    totals, backs, carried = [], [], ()

    def move(part, carried):
        return move_chunks(
            end_flag, share, totals[part], backs[part], flat, flat_v,
            places[part.start], sizes[part], carried,
        )

    for chunk in range(count):
        got = send(own[chunk], TO_MIDS)
        if chunk >= 2:
            got = tie(got, totals[chunk - 2])
        total = own[chunk] + got
        total = total + send(total, ACROSS)
        if chunk in early:
            total = tie(total, early[chunk])
        if chunk == count - 3:
            carried = move(groups[0], carried)
            total = tie(total, carried[1])
        totals.append(total)
        backs.append(send(total, TO_ENDS))
    carried = move(groups[1], carried)
    for part in groups[2:]:
        carried = move(part, carried)
    spread_v = next_spread_v
    flat_v = carried[0]
    line_v = flat_v.reshape(line_v.shape)
    spread_sq = lax.optimization_barrier(jnp.sum(spread_sq, axis=(1, 2)))
    factor, line_factor = factors(spread_sq + placed(jnp.sum(carried[1], axis=(1, 2))))

    order = [jnp.where(is_low, LINE - 1 - place, place) for place in range(LINE)]
    block = step_blocks(order[:1], line_factor, held, line_v)
    block += step_blocks(order[1:], line_factor, held, tie(line_v, block[0]))
    arrived = [send(block[place], TO_MIDS) for place in range(3)]
    passed = [send(block[place] + arrived[place], ACROSS) for place in range(2)]
    last = send(block[3] + passed[0], TO_ENDS)
    own_v = lax.dynamic_index_in_dim(line_v, o, 0, keepdims=False)
    own_v = lax.optimization_barrier(own_v + jnp.where(is_end, block[3], block[2]) * share)
    own_v = own_v + jnp.where(is_end, last, arrived[2] + passed[1]) * share
    step = jnp.sum(factor[:, None, None] * (spread - spread_v[None]), axis=0)
    buffer = lax.optimization_barrier(jnp.pad(spread_v + step * share, ((0, rest), (0, 0))))
    return lax.dynamic_update_slice(buffer, own_v, (cut, 0))


def solution(mesh):
    in_specs = (P("worker", "outer", None, "mp"), P(("worker", "outer"), "mp"), P())
    out_specs = P(("worker", "outer"), "mp")

    return jax.shard_map(on_device, mesh=mesh, in_specs=in_specs, out_specs=out_specs, check_vma=False)
```
